256 devices in a mesh: region: 4 (over x), blk: 64 (over z, y, core).
Axes of the slice: x: 4, y: 4, z: 8, core: 2. Of those that a mesh axis runs over, the one named last changes fastest.
Arguments:
- click_field: float32 [512, 32, 32, 128], P(('region', 'blk')), parts along dimension 0, may hold values from -360 to 360
- roughness: float32 [512, 32, 128], P(('region', 'blk')), parts along dimension 0, may hold values from 0.5 to 2
- slot_block: int32 [512], P('region'), parts along dimension 0, may hold values from -1 to 63, as said below
- neighbours: int32 [256, 4], P('region'), parts along dimension 0, may hold values from -1 to 63, as said below
- density: int32 [256], P('region'), parts along dimension 0, may hold values from 0 to 3
- class_kappa: float32 [4], replicated, may hold values from 0.1 to 2
Outputs:
- smoothed: float32 [512, 32, 32, 128], P(('region', 'blk')), parts along dimension 0
The draws below stay inside these ranges and needn't reach their ends.
There are 4 independent parts, one for each index of `region`. The reference program is written for one: setup_inputs(seed, part) draws one part's arguments, and reference() takes and returns one part's arrays. A program takes and returns all parts, laid end to end along the dimension named above; an argument that names none is the same for every part. Nothing has to cross between parts.
Inputs may be any that keep to these rules, and one draw needn't show every extreme that they name: `slot_block`: each of the 64 block ids sits in exactly one slot, -1 marks an empty slot, and ids rise along the filled slots; in each aligned group of four devices along blk one holds 2 blocks, one holds none and two hold one, and the group half the axis further along blk has the same arrangement. `neighbours`: block b lies in column b % 8 of a 8 x 8 grid, or in column 7 - b % 8 for all blocks as drawn, and in row 2 (b // 8) when b // 8 < 4, else in row 2 (b // 8) - 7; row b names the blocks beside b to the west, east, north and south, -1 at the region's edge and where the link between two blocks beside each other in a grid row is cut; the lists agree with one another.
All inputs are finite; a program needn't handle non-finite values.
Results may differ from the reference program's by a relative error of at most 0.0003.
Values may be sent and summed in bfloat16 or wider, within the bound.
A program may use at most 64 MiB of HBM per device.

```python
import math
import jax
import jax.numpy as jnp
from jax import lax

CATEGORY_FIELDS = 32
BLOCK_SIDE_CELLS = 128
BLOCK_ROWS = 32
DEVICE_SLOTS = 2
ITERS = 2
CLASSES = 4
BLOCKS = 64
GX = 8
GY = 8
REGION_SLOTS = 128


def shared_layout(key):
    mirror_key, cut_key, turn_key, flip_key = jax.random.split(jax.random.fold_in(key, 11), 4)
    mirror_x = jax.random.randint(mirror_key, (), 0, 2).astype(jnp.int32)
    block_ids = jnp.arange(BLOCKS, dtype=jnp.int32)
    half_rows = GY // 2
    id_row = block_ids // GX
    id_col = block_ids % GX
    grid_row = jnp.where(id_row < half_rows, 2 * id_row, 2 * (id_row - half_rows) + 1)
    grid_col = jnp.where(mirror_x == 1, GX - 1 - id_col, id_col)

    def id_at(row_at, col_at):
        back_row = jnp.where(row_at % 2 == 0, row_at // 2, row_at // 2 + half_rows)
        back_col = jnp.where(mirror_x == 1, GX - 1 - col_at, col_at)
        return back_row * GX + back_col
    cuts = jax.random.randint(cut_key, (GY, GX), 0, 2).astype(jnp.int32)
    west_cut = cuts[grid_row, jnp.clip(grid_col - 1, 0, GX - 1)]
    east_cut = cuts[grid_row, grid_col]
    west_ok = (grid_col > 0) & (west_cut == 0)
    east_ok = (grid_col < GX - 1) & (east_cut == 0)
    north_ok = grid_row > 0
    south_ok = grid_row < GY - 1
    to_west = jnp.where(west_ok, id_at(grid_row, grid_col - 1), -1)
    to_east = jnp.where(east_ok, id_at(grid_row, grid_col + 1), -1)
    to_north = jnp.where(north_ok, id_at(grid_row - 1, grid_col), -1)
    to_south = jnp.where(south_ok, id_at(grid_row + 1, grid_col), -1)
    near_lists = jnp.stack([to_west, to_east, to_north, to_south], axis=1).astype(jnp.int32)
    device_count = REGION_SLOTS // DEVICE_SLOTS
    groups = device_count // 4
    half_groups = groups // 2
    turns_half = jax.random.randint(turn_key, (half_groups,), 0, 4).astype(jnp.int32)
    mirrors_half = jax.random.randint(flip_key, (half_groups,), 0, 2).astype(jnp.int32)
    turns = jnp.concatenate([turns_half, turns_half])
    mirrors = jnp.concatenate([mirrors_half, mirrors_half])
    inner = jnp.arange(4, dtype=jnp.int32)
    place = jnp.where(mirrors[:, None] == 1, 3 - inner[None, :], inner[None, :])
    pattern_pos = (place + turns[:, None]) % 4
    counts = jnp.where(pattern_pos == 0, DEVICE_SLOTS, jnp.where(pattern_pos == 1, 0, 1)).reshape(-1).astype(jnp.int32)
    offsets = jnp.cumsum(counts) - counts
    slot_pos = jnp.arange(DEVICE_SLOTS, dtype=jnp.int32)
    filled = slot_pos[None, :] < counts[:, None]
    dealt = jnp.where(filled, offsets[:, None] + slot_pos[None, :], -1).reshape(-1).astype(jnp.int32)
    return (dealt, near_lists)


def draw_slot_block(key, part):
    return shared_layout(key)[0]


def draw_neighbours(key, part):
    return shared_layout(key)[1]


def draw_click_field(key, part):
    noise_key, scale_key = jax.random.split(key, 2)
    tensor_dims = (REGION_SLOTS, CATEGORY_FIELDS, BLOCK_ROWS, BLOCK_SIDE_CELLS)
    slot_sequence = 3.0 ** (jnp.arange(REGION_SLOTS, dtype=jnp.float32) / max(REGION_SLOTS - 1, 1))
    spread = jnp.exp(jax.random.uniform(scale_key, (CATEGORY_FIELDS,), jnp.float32, 0.0, math.log(10.0)))
    raw_noise = jnp.clip(jax.random.normal(noise_key, tensor_dims, jnp.float32), -6.0, 6.0)
    return 2.0 * raw_noise * spread[None, :, None, None] * slot_sequence[:, None, None, None]


def plant(entries, key, smallest, high):
    spot = [jax.random.randint(jax.random.fold_in(key, axis), (), 0, length) for axis, length in enumerate(entries.shape)]
    main_axis = entries.shape.index(max(entries.shape))
    next_to = spot[:main_axis] + [(spot[main_axis] + 1) % entries.shape[main_axis]] + spot[main_axis + 1:]
    return entries.at[tuple(spot)].set(smallest).at[tuple(next_to)].set(high)


def levels(rng, dims, pieces, smallest, largest):
    loudness, own = 1.0, jax.random.fold_in(rng, 6)
    for dim, blocks in pieces:
        steps = jnp.exp(jax.random.uniform(jax.random.fold_in(own, dim), (blocks,), jnp.float32, smallest / len(pieces), largest / len(pieces)))
        loudness = loudness * jnp.repeat(steps, dims[dim] // blocks).reshape([-1 if axis == dim else 1 for axis in range(len(dims))])
    return loudness


def setup_inputs(seed: int = 0, part: int = 0) -> dict:
    streams_of = jax.random.split(jax.random.key(seed), 7)
    part_splits = jax.random.split(jax.random.fold_in(streams_of[6], part), 7)
    click_field = draw_click_field(jax.random.fold_in(jax.random.fold_in(streams_of[6], part), 71), part)
    roughness = jnp.clip(jnp.exp(math.log(2.0) - 1.3862944 * jax.random.uniform(part_splits[1], (REGION_SLOTS, BLOCK_ROWS, BLOCK_SIDE_CELLS), jnp.float32) ** levels(part_splits[1], (REGION_SLOTS, BLOCK_ROWS, BLOCK_SIDE_CELLS), ((0, 64),), -0.2, 0.2)), 0.5, 2.0)
    slot_block = draw_slot_block(jax.random.fold_in(jax.random.fold_in(streams_of[6], part), 71), part)
    neighbours = draw_neighbours(jax.random.fold_in(jax.random.fold_in(streams_of[6], part), 71), part)
    density = plant(jax.random.randint(part_splits[4], (BLOCKS,), 0, CLASSES), jax.random.fold_in(part_splits[4], 1), 0, CLASSES - 1).astype(jnp.int32)
    class_kappa = jnp.clip(jnp.exp(jax.random.uniform(streams_of[5], (CLASSES,), jnp.float32, math.log(0.1), math.log(2.0))), 0.1, 2.0)
    return dict(click_field=click_field, roughness=roughness, slot_block=slot_block, neighbours=neighbours, density=density, class_kappa=class_kappa)


def edge_strips(values):
    upright = jnp.stack([values[..., 0], values[..., -1]], axis=1).astype(jnp.bfloat16)
    level = jnp.stack([values[:, :, 0, :], values[:, :, -1, :]], axis=1).astype(jnp.bfloat16)
    return (upright, level)

def stencil(values, kappa_sq, upright, level):
    side_cols = upright.astype(jnp.float32)
    side_rows = level.astype(jnp.float32)
    from_west = jnp.concatenate([side_cols[:, 0][..., None], values[..., :-1]], axis=-1)
    from_east = jnp.concatenate([values[..., 1:], side_cols[:, 1][..., None]], axis=-1)
    from_north = jnp.concatenate([side_rows[:, 0][:, :, None, :], values[:, :, :-1, :]], axis=2)
    from_south = jnp.concatenate([values[:, :, 1:, :], side_rows[:, 1][:, :, None, :]], axis=2)
    return (kappa_sq[:, None] + 4.0) * values - (from_west + from_east + from_north + from_south)

def gram_of(first_field, second_field):
    return jnp.einsum('nfyx,ngyx->fg', first_field, second_field, precision=lax.Precision.HIGHEST)

def combine(values, mixing):
    return jnp.einsum('nfyx,fg->ngyx', values, mixing, precision=lax.Precision.HIGHEST)

def spd_solve(matrix, targets):
    balanced = 0.5 * (matrix + matrix.T)
    factor = jnp.linalg.cholesky(balanced)
    return jax.scipy.linalg.cho_solve((factor, True), targets)

def reference(click_field, roughness, slot_block, neighbours, density, class_kappa):
    block_ids = jnp.arange(BLOCKS, dtype=jnp.int32)
    slot_numbers = jnp.arange(REGION_SLOTS, dtype=jnp.int32)
    slot_of = jnp.sum(jnp.where(slot_block[None, :] == block_ids[:, None], slot_numbers[None, :], 0), axis=1).astype(jnp.int32)
    sources = click_field[slot_of]
    kappa_sq = class_kappa[density][:, None, None] * roughness[slot_of]
    facing = jnp.array([1, 0], jnp.int32)
    present = neighbours >= 0
    safe_near = jnp.clip(neighbours, 0, BLOCKS - 1).astype(jnp.int32)

    def fetch_borders(values):
        upright, level = edge_strips(values)
        side_cols = upright[safe_near[:, :2], facing[None, :]]
        side_rows = level[safe_near[:, 2:], facing[None, :]]
        side_cols = jnp.where(present[:, :2, None, None], side_cols, jnp.zeros_like(side_cols))
        side_rows = jnp.where(present[:, 2:, None, None], side_rows, jnp.zeros_like(side_rows))
        return (side_cols, side_rows)

    def operate(values):
        cols_one, rows_one = fetch_borders(values)
        first_pass = stencil(values, kappa_sq, cols_one, rows_one)
        cols_two, rows_two = fetch_borders(first_pass)
        return stencil(first_pass, kappa_sq, cols_two, rows_two)
    residual = sources
    direction = sources
    solution = jnp.zeros_like(sources)
    norm_now = gram_of(residual, residual)
    for iteration in range(ITERS):
        applied = operate(direction)
        step_size = spd_solve(gram_of(direction, applied), norm_now)
        solution = solution + combine(direction, step_size)
        residual = residual - combine(applied, step_size)
        if iteration + 1 < ITERS:
            norm_next = gram_of(residual, residual)
            carry_over = spd_solve(norm_now, norm_next)
            direction = residual + combine(direction, carry_over)
            norm_now = norm_next
    filled = slot_block >= 0
    placed = solution[jnp.clip(slot_block, 0, BLOCKS - 1).astype(jnp.int32)]
    return jnp.where(filled[:, None, None, None], placed, jnp.zeros_like(placed))
```

```python
import jax
import jax.numpy as jnp
from jax import lax
from jax.experimental import pallas as pl
from jax.experimental.pallas import tpu as pltpu
from jax.sharding import PartitionSpec as P

F32, BF16 = jnp.float32, jnp.bfloat16
MESH = pl.DeviceIdType.MESH
LEVELS = 3


def lanes(rows):
    return lax.broadcasted_iota(jnp.int32, (rows, 128), 1)


def roll(value, shift):
    return value if shift % 128 == 0 else pltpu.roll(value, shift % 128, 1)


def split(value):
    high = value.astype(BF16)
    low = (value - high.astype(F32)).astype(BF16)
    return high, low


def kernel(
    slots, near, density, kappas, field, rough, out,
    staged, result, cell_b, cell_v, cell_q, diag, halves_b, halves_q, halves,
    send_rows, send_cols, rows_0, rows_1, rows_2, cols_0, cols_1, cols_2, grams, sum_plane, part_z, sum_z,
    in_sem, out_sem, row_send, row_recv, col_send, col_recv, plane_send, plane_recv, z_send, z_recv,
):
    recv_rows, recv_cols = (rows_0, rows_1, rows_2), (cols_0, cols_1, cols_2)
    region, me = lax.axis_index("region"), lax.axis_index("blk")
    depth, spot = me // 8, me % 8
    half, inner = spot // 4, spot % 4
    low_half = depth < 4
    straight = lax.rem(me + 32, 64)
    crossing = jnp.where(depth == 0, 7, jnp.where(depth == 7, 0, jnp.where(low_half, depth + 3, depth - 3)))

    def device(number):
        return (region, number)

    def in_plane(step):
        return depth * 8 + lax.rem(spot + step, 8)

    def in_crossing(step):
        return crossing * 8 + half * 4 + lax.rem(inner + step, 4)

    def along_z(step):
        return lax.rem(depth + step, 8) * 8 + spot

    load = [pltpu.make_async_copy(field.at[pl.ds(s * 1024, 1024)], staged.at[pl.ds(s * 1024, 1024)], in_sem.at[s]) for s in range(2)]
    for copy in load:
        copy.start()

    barrier = pltpu.get_barrier_semaphore()
    peers = [in_plane(k) for k in range(1, 8)] + [along_z(k) for k in range(1, 8)] + [in_crossing(k) for k in range(1, 4)]
    for peer in peers:
        pl.semaphore_signal(barrier, inc=1, device_id=device(peer), device_id_type=MESH)

    blocks = [slots[me * 2 + s] for s in range(2)]
    filled = [b >= 0 for b in blocks]
    safe = [jnp.maximum(b, 0) for b in blocks]
    kappa = [kappas[density[b]] for b in safe]
    sides = [[jnp.where(filled[s], near[safe[s], k], -1) for k in range(4)] for s in range(2)]
    plane_ids = [slots[depth * 16 + u] for u in range(16)]
    cross_ids = [slots[(crossing * 2 + half) * 8 + u] for u in range(8)]
    straight_ids = [slots[straight * 2 + u] for u in range(2)]

    def find(block, ids):
        place = jnp.int32(0)
        for u, candidate in enumerate(ids):
            place = jnp.where(candidate == block, u, place)
        return place

    col_at, row_at = [], []
    for s in range(2):
        cols = []
        for k in range(2):
            u = find(sides[s][k], plane_ids)
            cols.append(((spot - (u >> 1)) & 7, u & 1))
        col_at.append(cols)
        north = jnp.where(low_half, sides[s][2], sides[s][3])
        south = jnp.where(low_half, sides[s][3], sides[s][2])
        u = find(north, cross_ids)
        cross_spot = ((inner - (u >> 1)) & 3) * 2 + (u & 1)
        straight_spot = 8 + find(south, straight_ids)
        row_at.append((jnp.where(low_half, cross_spot, straight_spot), jnp.where(low_half, straight_spot, cross_spot)))

    def row_copies(level):
        crossing_side = jnp.where(low_half, 0, 1)
        copies = [
            pltpu.make_async_remote_copy(
                send_rows.at[level, crossing_side],
                recv_rows[level].at[pl.ds(2 * k, 2)],
                row_send.at[level, k], row_recv.at[level, k],
                device_id=device(in_crossing(k)), device_id_type=MESH)
            for k in range(4)
        ]
        copies.append(pltpu.make_async_remote_copy(
            send_rows.at[level, 1 - crossing_side],
            recv_rows[level].at[pl.ds(8, 2)],
            row_send.at[level, 4], row_recv.at[level, 4],
            device_id=device(straight), device_id_type=MESH))
        return copies

    def col_copies(level):
        return [
            pltpu.make_async_remote_copy(
                send_cols.at[level], recv_cols[level].at[k],
                col_send.at[level, k], col_recv.at[level, k],
                device_id=device(in_plane(k)), device_id_type=MESH)
            for k in range(1, 8)
        ]

    lane32, lane128 = lanes(32), lanes(128)

    def post_edges(cells, level):
        for s in range(2):
            for side, slab in ((0, 1), (1, 8)):
                packed = jnp.zeros((32, 128), F32)
                for k in range(4):
                    piece = roll(cells[s, slab, 8 + 32 * k:40 + 32 * k, :], 32 * k - 96 * side)
                    packed = jnp.where((lane32 >> 5) == k, piece, packed)
                send_rows[level, side, s] = packed.astype(BF16)
            west = [cells[s, 1 + y, 8:9, :] for y in range(8)]
            east = [cells[s, 1 + y, 135:136, :] for y in range(8)]
            strip = jnp.concatenate(west + east, axis=0).astype(BF16)
            send_cols[level, s] = strip
            recv_cols[level][0, s] = strip

    def start_edges(level):
        for copy in row_copies(level) + col_copies(level):
            copy.start()

    def wait_edges(level):
        for copy in col_copies(level) + row_copies(level):
            copy.wait_recv()

    def apply_edges(cells, level):
        for s in range(2):
            for k, row in ((0, 8), (1, 135)):
                step, slot = col_at[s][k]
                strip = recv_cols[level][step, slot].astype(F32)
                strip = strip[8:16] if k == 0 else strip[0:8]
                strip = jnp.where(sides[s][k] >= 0, strip, 0.0)
                for y in range(8):
                    cells[s, 1 + y, row:row + 1, :] = cells[s, 1 + y, row:row + 1, :] - strip[y:y + 1]
            for side, slab in ((0, 1), (1, 8)):
                strip = recv_rows[level][row_at[s][side]].astype(F32)
                strip = jnp.where(sides[s][2 + side] >= 0, strip, 0.0)
                touching = (lane32 >> 5) == 3 * side
                for k in range(4):
                    rows = slice(8 + 32 * k, 40 + 32 * k)
                    piece = jnp.where(touching, roll(strip, 96 * side - 32 * k), 0.0)
                    cells[s, slab, rows, :] = cells[s, slab, rows, :] - piece

    def wrap(cells):
        for s in range(2):
            cells[s, 0, 8:136, :] = jnp.where(lane128 < 32, 0.0, roll(cells[s, 8, 8:136, :], 32))
            cells[s, 9, 8:136, :] = jnp.where(lane128 >= 96, 0.0, roll(cells[s, 1, 8:136, :], 96))

    def each_slab(body):
        def step(i, carry):
            body(i >> 3, i & 7)
            return carry
        lax.fori_loop(0, 16, step, 0)

    def operate(source, target):
        def body(s, y):
            centre = source[s, y + 1, 8:136, :]
            beside = source[s, y + 1, 7:135, :] + source[s, y + 1, 9:137, :]
            along = source[s, y, 8:136, :] + source[s, y + 2, 8:136, :]
            target[s, y + 1, 8:136, :] = diag[s, y] * centre - (beside + along)
        each_slab(body)

    def gram(cells, parts):
        def body(s, y):
            high, low = split(cells[s, y + 1, 8:136, :])
            row = pl.ds(pl.multiple_of(y * 128, 128), 128)
            parts[s, row, 0:128] = high
            parts[s, row, 128:256] = low
        each_slab(body)
        total = jnp.zeros((128, 256), F32)
        for s in range(2):
            total = total + lax.dot_general(
                parts[s, :, 0:128], parts[s], (((0,), (0,)), ((), ())), preferred_element_type=F32)
        total = total[:, 0:128] + 2.0 * total[:, 128:256]
        answer = total[0:32]
        for k in range(1, 4):
            answer = answer + roll(total[32 * k:32 * k + 32], -32 * k)
        return jnp.where(lane32 < 32, answer, 0.0)

    blank = jnp.zeros((8, 128), F32)
    for cells in (cell_b, cell_v, cell_q):
        for s in range(2):
            for y in range(10):
                cells[s, y, 0:8, :] = blank
                cells[s, y, 136:144, :] = blank

    def fill_diag(s, y):
        value = jnp.where(s == 0, kappa[0], kappa[1])
        rows = [jnp.broadcast_to(rough[pl.ds(s * 32 + k * 8 + y, 1), :], (32, 128)) for k in range(4)]
        diag[s, y] = jnp.transpose(jnp.concatenate(rows, axis=0)) * value + 4.0
    each_slab(fill_diag)

    for copy in load:
        copy.wait()

    def turn(s, y):
        keep = jnp.where(s == 0, blocks[0], blocks[1]) >= 0
        rows = [staged[pl.ds(s * 1024 + k * 8 + y, 32, stride=32), :] for k in range(4)]
        cell_b[s, y + 1, 8:136, :] = jnp.where(keep, jnp.transpose(jnp.concatenate(rows, axis=0)), 0.0)
    each_slab(turn)

    post_edges(cell_b, 0)
    pl.semaphore_wait(barrier, len(peers))
    start_edges(0)
    wrap(cell_b)
    operate(cell_b, cell_v)
    gram_s = gram(cell_b, halves_b)
    wait_edges(0)
    apply_edges(cell_v, 0)
    post_edges(cell_v, 1)
    start_edges(1)
    wrap(cell_v)
    operate(cell_v, cell_q)
    gram_g = gram(cell_v, halves)
    wait_edges(1)
    apply_edges(cell_q, 1)
    post_edges(cell_q, 2)
    start_edges(2)
    wrap(cell_q)
    operate(cell_q, cell_v)
    gram_h = gram(cell_q, halves_q)
    wait_edges(2)
    apply_edges(cell_v, 2)
    gram_y = gram(cell_v, halves)

    own = gram_s + roll(gram_g, 32) + roll(gram_h, 64) + roll(gram_y, 96)
    grams[...] = own
    plane_copies = [
        pltpu.make_async_remote_copy(
            grams, sum_plane.at[k], plane_send.at[k], plane_recv.at[k],
            device_id=device(in_plane(k)), device_id_type=MESH)
        for k in range(1, 8)
    ]
    for copy in plane_copies:
        copy.start()
    for k, copy in enumerate(plane_copies):
        copy.wait_recv()
        own = own + sum_plane[k + 1]
    part_z[...] = own
    z_copies = [
        pltpu.make_async_remote_copy(
            part_z, sum_z.at[k], z_send.at[k], z_recv.at[k],
            device_id=device(along_z(k)), device_id_type=MESH)
        for k in range(1, 8)
    ]
    for copy in z_copies:
        copy.start()
    for k, copy in enumerate(z_copies):
        copy.wait_recv()
        own = own + sum_z[k + 1]

    turned = jnp.transpose(jnp.concatenate([own, jnp.zeros((96, 128), F32)], axis=0))
    s_mat, g_mat, h_mat, y_mat = [
        jnp.where(lane32 < 32, 0.5 * (roll(own, -32 * m) + turned[32 * m:32 * m + 32]), 0.0) for m in range(4)
    ]
    system = jnp.concatenate([
        g_mat + roll(h_mat, 32) + roll(s_mat, 64),
        h_mat + roll(y_mat, 32) + roll(g_mat, 64),
    ], axis=0)
    row_id = lax.broadcasted_iota(jnp.int32, (64, 128), 0)
    for k in range(64):
        pivot = system[k:k + 1, :] / system[k:k + 1, k:k + 1]
        system = jnp.where(row_id == k, pivot, system - system[:, k:k + 1] * pivot)
    mix = roll(jnp.where((lanes(64) >> 5) == 2, system, 0.0), 64)
    mix = mix + roll(mix, 32) + roll(mix, 64) + roll(mix, 96)
    pieces = [jnp.where((lane32 >> 5) == k, mix[32 * m:32 * m + 32], 0.0) for m in range(2) for k in range(4)]
    weights = jnp.concatenate([
        jnp.transpose(jnp.concatenate(pieces[0:4], axis=0)),
        jnp.transpose(jnp.concatenate(pieces[4:8], axis=0)),
    ], axis=1)
    weight_high, weight_low = split(weights)
    weight_both = jnp.concatenate([weight_high, weight_low], axis=0)
    across = (((1,), (1,)), ((), ()))

    def finish(s, y):
        row = pl.ds(pl.multiple_of(y * 128, 128), 128)
        high = jnp.concatenate([halves_b[s, row, 0:128], halves_q[s, row, 0:128]], axis=1)
        low = jnp.concatenate([halves_b[s, row, 128:256], halves_q[s, row, 128:256]], axis=1)
        first = lax.dot_general(weight_both, high, across, preferred_element_type=F32)
        second = lax.dot_general(weight_high, low, across, preferred_element_type=F32)
        value = first[0:128] + first[128:256] + second
        for k in range(4):
            result[pl.ds(s * 1024 + k * 8 + y, 32, stride=32), :] = value[32 * k:32 * k + 32]
    each_slab(finish)
    store = pltpu.make_async_copy(result, out, out_sem)
    store.start()
    for level in range(LEVELS):
        for copy in row_copies(level) + col_copies(level):
            copy.wait_send()
    for copy in plane_copies + z_copies:
        copy.wait_send()
    store.wait()


def on_device(click_field, roughness, slot_block, neighbours, density, class_kappa):
    smem = pl.BlockSpec(memory_space=pltpu.SMEM)
    vmem = pl.BlockSpec(memory_space=pltpu.VMEM)
    anywhere = pl.BlockSpec(memory_space=pl.ANY)
    dma = pltpu.SemaphoreType.DMA
    answer = pl.pallas_call(
        kernel,
        out_shape=jax.ShapeDtypeStruct((2048, 128), F32),
        in_specs=[smem, smem, smem, smem, anywhere, vmem],
        out_specs=anywhere,
        scratch_shapes=[
            pltpu.VMEM((2048, 128), F32),
            pltpu.VMEM((2048, 128), F32),
            pltpu.VMEM((2, 10, 144, 128), F32),
            pltpu.VMEM((2, 10, 144, 128), F32),
            pltpu.VMEM((2, 10, 144, 128), F32),
            pltpu.VMEM((2, 8, 128, 128), F32),
            pltpu.VMEM((2, 1024, 256), BF16),
            pltpu.VMEM((2, 1024, 256), BF16),
            pltpu.VMEM((2, 1024, 256), BF16),
            pltpu.VMEM((LEVELS, 2, 2, 32, 128), BF16),
            pltpu.VMEM((LEVELS, 2, 16, 128), BF16),
            *[pltpu.VMEM((10, 32, 128), BF16) for _ in range(LEVELS)],
            *[pltpu.VMEM((8, 2, 16, 128), BF16) for _ in range(LEVELS)],
            pltpu.VMEM((32, 128), F32),
            pltpu.VMEM((8, 32, 128), F32),
            pltpu.VMEM((32, 128), F32),
            pltpu.VMEM((8, 32, 128), F32),
            dma((2,)), dma,
            dma((LEVELS, 5)), dma((LEVELS, 5)),
            dma((LEVELS, 8)), dma((LEVELS, 8)),
            dma((8,)), dma((8,)), dma((8,)), dma((8,)),
        ],
        compiler_params=pltpu.CompilerParams(
            collective_id=0, has_side_effects=True, vmem_limit_bytes=40 * 1024 * 1024),
        name="smooth",
    )(
        slot_block, neighbours, density, class_kappa,
        click_field.reshape(2048, 128), roughness.reshape(64, 128),
    )
    return answer.reshape(click_field.shape)


def solution(mesh):
    return jax.shard_map(
        on_device,
        mesh=mesh,
        in_specs=(
            P(("region", "blk"), None, None, None),
            P(("region", "blk"), None, None),
            P("region"),
            P("region", None),
            P("region"),
            P(),
        ),
        out_specs=P(("region", "blk"), None, None, None),
        check_vma=False,
    )
```

```python
import jax
import jax.numpy as jnp
from jax import lax
from jax.experimental import pallas as pl
from jax.experimental.pallas import tpu as pltpu
from jax.sharding import PartitionSpec as P

F32, BF16 = jnp.float32, jnp.bfloat16
MESH = pl.DeviceIdType.MESH


def lanes(rows):
    return lax.broadcasted_iota(jnp.int32, (rows, 128), 1)


def roll(value, shift):
    return value if shift % 128 == 0 else pltpu.roll(value, shift % 128, 1)


def split(value):
    high = value.astype(BF16)
    low = (value - high.astype(F32)).astype(BF16)
    return high, low


def kernel(
    slots_in, near_in, density_in, kappas_in, field, rough_in, result,
    slots, near, density, kappas, rough,
    staged, cell_b, cell_v, cell_q, diag, halves_b, halves_q, halves,
    send_rows, send_cols_0, send_cols_1, rows_b, rows_v, rows_q, cols_0, cols_1, send_relay, relays,
    part_a, plane_a, mid_a, depth_a, part_b, plane_b, mid_b, depth_b,
    table_sem, in_sem, row_send, row_recv, col_send, col_recv, relay_send, relay_recv, sum_send, sum_recv,
):
    send_cols, recv_cols = (send_cols_0, send_cols_1), (cols_0, cols_1)
    recv_rows = (rows_b, rows_v, rows_q)
    region, me = lax.axis_index("region"), lax.axis_index("blk")
    depth, spot = me // 8, me % 8
    half, inner = spot // 4, spot % 4
    low_half = depth < 4
    straight = lax.rem(me + 32, 64)
    crossing = jnp.where(depth == 0, 7, jnp.where(depth == 7, 0, jnp.where(low_half, depth + 3, depth - 3)))

    def device(number):
        return (region, number)

    def in_plane(step):
        return depth * 8 + lax.rem(spot + step, 8)

    def in_crossing(step):
        return crossing * 8 + half * 4 + lax.rem(inner + step, 4)

    def along_z(step):
        return lax.rem(depth + step, 8) * 8 + spot

    tables = [
        pltpu.make_async_copy(source, target, table_sem.at[i])
        for i, (source, target) in enumerate((
            (slots_in, slots), (near_in, near), (density_in, density), (kappas_in, kappas), (rough_in, rough)))
    ]
    for copy in tables:
        copy.start()
    load = [pltpu.make_async_copy(field.at[pl.ds(s * 1024, 1024)], staged.at[pl.ds(s * 1024, 1024)], in_sem.at[s]) for s in range(2)]
    for copy in load:
        copy.start()

    barrier = pltpu.get_barrier_semaphore()
    peers = [in_plane(k) for k in range(1, 8)] + [along_z(k) for k in range(1, 8)] + [in_crossing(k) for k in range(1, 4)]
    for peer in peers:
        pl.semaphore_signal(barrier, inc=1, device_id=device(peer), device_id_type=MESH)

    for copy in tables:
        copy.wait()
    blocks = [slots[me * 2 + s] for s in range(2)]
    filled = [b >= 0 for b in blocks]
    safe = [jnp.maximum(b, 0) for b in blocks]
    kappa = [kappas[density[b]] for b in safe]
    sides = [[jnp.where(filled[s], near[k, safe[s]], -1) for k in range(4)] for s in range(2)]
    plane_ids = [slots[depth * 16 + u] for u in range(16)]
    cross_ids = [slots[(crossing * 2 + half) * 8 + u] for u in range(8)]
    straight_ids = [slots[straight * 2 + u] for u in range(2)]

    def find(block, ids):
        place = jnp.int32(0)
        for u, candidate in enumerate(ids):
            place = jnp.where(candidate == block, u, place)
        return place

    def look(side, block):
        return jnp.where(block >= 0, near[side, jnp.maximum(block, 0)], -1)

    def first_of(*choices):
        answer = choices[-1]
        for choice in choices[-2::-1]:
            answer = jnp.where(choice >= 0, choice, answer)
        return answer

    def plane_place(block):
        u = find(block, plane_ids)
        return (spot - (u >> 1)) & 7, u & 1

    col_at, row_at, flank_at, relay_at, corner = [], [], [], [], []
    for s in range(2):
        here, north, south = blocks[s], sides[s][2], sides[s][3]
        col_at.append([plane_place(sides[s][k]) for k in range(2)])
        flank_at.append([
            plane_place(first_of(sides[s][k], look(3, look(k, north)), look(2, look(k, south)))) for k in range(2)
        ])
        far = jnp.where(low_half, north, south)
        close = jnp.where(low_half, south, north)
        u, v = find(far, cross_ids), find(close, straight_ids)
        far_step, far_slot = (inner - (u >> 1)) & 3, u & 1
        spots = (u, 8 + v)
        places = ((far_step, far_slot), (jnp.int32(4), v))
        row_at.append((jnp.where(low_half, spots[0], spots[1]), jnp.where(low_half, spots[1], spots[0])))
        relay_at.append([
            tuple(jnp.where(low_half, places[side][i], places[1 - side][i]) for i in range(2)) for side in range(2)
        ])
        corner.append([[
            jnp.where(beyond >= 0, jnp.where(look(k, beyond) >= 0, 1.0, 0.0) + jnp.where(sides[s][k] >= 0, 1.0, 0.0), 0.0)
            for k in range(2)] for beyond in (north, south)])

    crossing_side = jnp.where(low_half, 0, 1)

    core, chip = inner % 2, inner // 2
    sibling = in_plane(1 - 2 * core + 8)

    def remote(source, target, send, recv, number):
        return pltpu.make_async_remote_copy(source, target, send, recv, device_id=device(number), device_id_type=MESH)

    def cross_copies(kind):
        source = send_rows.at[kind, crossing_side]
        target = recv_rows[kind].at[pl.ds(2 * inner, 2)]
        return [
            remote(source, target, row_send.at[kind, k], row_recv.at[kind, chip],
                   crossing * 8 + half * 4 + 2 * k + core)
            for k in range(2)
        ]

    def cross_waits(kind):
        return [
            remote(send_rows.at[kind, crossing_side], recv_rows[kind].at[pl.ds(2 * (2 * k + core), 2)],
                   row_send.at[kind, k], row_recv.at[kind, k], sibling)
            for k in range(2)
        ]

    def straight_copies(kind):
        return [remote(send_rows.at[kind, 1 - crossing_side], recv_rows[kind].at[pl.ds(8, 2)],
                       row_send.at[kind, 2], row_recv.at[kind, 2], straight)]

    def hand_copies(kind):
        return [
            remote(recv_rows[kind].at[pl.ds(2 * (2 * k + core), 2)], recv_rows[kind].at[pl.ds(2 * (2 * k + core), 2)],
                   row_send.at[kind, 3 + k], row_recv.at[kind, 3 + k], sibling)
            for k in range(2)
        ]

    def hand_waits(kind):
        return [
            remote(recv_rows[kind].at[pl.ds(2 * (2 * k + core), 2)], recv_rows[kind].at[pl.ds(2 * (2 * k + 1 - core), 2)],
                   row_send.at[kind, 3 + k], row_recv.at[kind, 3 + k], sibling)
            for k in range(2)
        ]

    def send_row_strips(kind):
        start(straight_copies(kind) + cross_copies(kind))

    def hand_on(kind):
        arrive(cross_waits(kind))
        start(hand_copies(kind))

    def relay_copies():
        return [
            remote(send_relay.at[crossing_side], relays.at[k], relay_send.at[k], relay_recv.at[k], in_crossing(k))
            for k in range(4)
        ] + [remote(send_relay.at[1 - crossing_side], relays.at[4], relay_send.at[4], relay_recv.at[4], straight)]

    def col_copies(level):
        return [
            pltpu.make_async_remote_copy(
                send_cols[level], recv_cols[level].at[k],
                col_send.at[level, k], col_recv.at[level, k],
                device_id=device(in_plane(k)), device_id_type=MESH)
            for k in range(1, 8)
        ]

    lane32, lane128 = lanes(32), lanes(128)

    sides_of_slab = ((0, 1), (1, 8))

    def packed(cells, s, side, slab):
        answer = jnp.zeros((32, 128), F32)
        for k in range(4):
            piece = roll(cells[s, slab, 8 + 32 * k:40 + 32 * k, :], 32 * k - 96 * side)
            answer = jnp.where((lane32 >> 5) == k, piece, answer)
        return answer.astype(BF16)

    def columns(cells, s):
        return [cells[s, 1 + y, row:row + 1, :] for row in (8, 135) for y in range(8)]

    def send_columns(level, s, rows):
        strip = jnp.concatenate(rows, axis=0).astype(BF16)
        send_cols[level][s] = strip
        recv_cols[level][0, s] = strip

    def start(copies):
        for copy in copies:
            copy.start()

    def arrive(copies):
        for copy in copies:
            copy.wait_recv()

    def linked(s, k):
        return sides[s][k] >= 0

    def column_of(level, s, k, first):
        step, slot = col_at[s][k]
        strip = recv_cols[level][step, slot].astype(F32)
        return strip[first + 8:first + 16] if k == 0 else strip[first:first + 8]

    def take_columns(cells, s, k, strip):
        row = (8, 135)[k]
        strip = jnp.where(linked(s, k), strip, 0.0)
        for y in range(8):
            cells[s, 1 + y, row:row + 1, :] = cells[s, 1 + y, row:row + 1, :] - strip[y:y + 1]

    def take_rows(cells, s, side, slab, strip, back=None):
        touching = (lane32 >> 5) == 3 * side
        for k in range(4):
            rows = slice(8 + 32 * k, 40 + 32 * k)
            piece = roll(strip, 96 * side - 32 * k)
            if back is not None:
                piece = piece - back[s, slab, rows, :]
            piece = jnp.where(touching, jnp.where(linked(s, 2 + side), piece, 0.0), 0.0)
            cells[s, slab, rows, :] = cells[s, slab, rows, :] - piece

    def send_relays():
        top = lax.broadcasted_iota(jnp.int32, (8, 128), 0)
        lane8 = lanes(8)
        found = []
        for s in range(2):
            (west_step, west_slot), (east_step, east_slot) = flank_at[s]
            found.append((
                recv_cols[0][west_step, west_slot].astype(F32)[8:16],
                recv_cols[0][east_step, east_slot].astype(F32)[0:8],
            ))
        for side in range(2):
            lines = []
            for west, east in found:
                row = slice(7 * side, 7 * side + 1)
                line = jnp.where(lanes(1) < 32, roll(west[row], 32 * side), roll(east[row], 32 + 32 * side))
                lines.append(jnp.broadcast_to(line, (8, 128)))
            value = jnp.where(top == 0, lines[0], lines[1])
            send_relay[side] = jnp.where(lane8 < 64, value, 0.0)
        start(relay_copies())

    def take_corners(cells):
        for s in range(2):
            for side, slab in sides_of_slab:
                index, slot = relay_at[s][side]
                tile = relays[index]
                line = jnp.where(slot == 0, tile[0:1], tile[1:2])
                for k, row in ((0, 8), (1, 135)):
                    factor = corner[s][side][k]
                    value = jnp.where(factor > 0.0, roll(line, 96 * side - 32 * k) * factor, 0.0)
                    value = jnp.where((lanes(1) >> 5) == 3 * side, value, 0.0)
                    cells[s, slab, row:row + 1, :] = cells[s, slab, row:row + 1, :] + value

    def wrap(cells):
        for s in range(2):
            cells[s, 0, 8:136, :] = jnp.where(lane128 < 32, 0.0, roll(cells[s, 8, 8:136, :], 32))
            cells[s, 9, 8:136, :] = jnp.where(lane128 >= 96, 0.0, roll(cells[s, 1, 8:136, :], 96))

    def each_slab(body, unroll=2):
        def step(i, carry):
            body(i >> 3, i & 7)
            return carry
        lax.fori_loop(0, 16, step, 0, unroll=unroll)

    def operate(source, target):
        def body(s, y):
            centre = source[s, y + 1, 8:136, :]
            beside = source[s, y + 1, 7:135, :] + source[s, y + 1, 9:137, :]
            along = source[s, y, 8:136, :] + source[s, y + 2, 8:136, :]
            target[s, y + 1, 8:136, :] = diag[s, y] * centre - (beside + along)
        each_slab(body)

    def multiply(parts, first, last):
        total = jnp.zeros((128, 256), F32)
        for s in range(2):
            rows = slice(first * 128, last * 128)
            total = total + lax.dot_general(
                parts[s, rows, 0:128], parts[s, rows, :], (((0,), (0,)), ((), ())), preferred_element_type=F32)
        return total

    def halve(cells, parts, s, y):
        high, low = split(cells[s, y + 1, 8:136, :])
        row = pl.ds(pl.multiple_of(y * 128, 128), 128)
        parts[s, row, 0:128] = high
        parts[s, row, 128:256] = low

    def fold(total):
        total = total[:, 0:128] + 2.0 * total[:, 128:256]
        answer = total[0:32]
        for k in range(1, 4):
            answer = answer + roll(total[32 * k:32 * k + 32], -32 * k)
        return jnp.where(lane32 < 32, answer, 0.0)

    def gram(cells, parts):
        each_slab(lambda s, y: halve(cells, parts, s, y))
        return fold(multiply(parts, 0, 8))

    def press(value):
        answer = value[0:8]
        for k in range(1, 4):
            answer = answer + roll(value[8 * k:8 * k + 8], 32 * k)
        return answer

    def spread(value):
        return jnp.concatenate([jnp.where(lanes(8) < 32, roll(value, -32 * k), 0.0) for k in range(4)], axis=0)

    def exchange(peer, source, target, index):
        return [
            pltpu.make_async_remote_copy(
                source, target.at[k], sum_send.at[index, k], sum_recv.at[index, k],
                device_id=device(peer(k)), device_id_type=MESH)
            for k in range(1, 8)
        ]

    def collect(copies, own, target):
        for k, copy in enumerate(copies):
            copy.wait_recv()
            own = own + target[k + 1]
        return own

    blank = jnp.zeros((8, 128), F32)
    for cells in (cell_b, cell_v, cell_q):
        for s in range(2):
            for y in range(10):
                cells[s, y, 0:8, :] = blank
                cells[s, y, 136:144, :] = blank

    def fill_diag(s, y):
        value = jnp.where(s == 0, kappa[0], kappa[1])
        rows = [jnp.broadcast_to(rough[pl.ds(s * 32 + k * 8 + y, 1), :], (32, 128)) for k in range(4)]
        diag[s, y] = jnp.transpose(jnp.concatenate(rows, axis=0)) * value + 4.0
    each_slab(fill_diag)

    for copy in load:
        copy.wait()

    def turn(s, y):
        keep = jnp.where(s == 0, blocks[0], blocks[1]) >= 0
        rows = [staged[pl.ds(s * 1024 + k * 8 + y, 32, stride=32), :] for k in range(4)]
        cell_b[s, y + 1, 8:136, :] = jnp.where(keep, jnp.transpose(jnp.concatenate(rows, axis=0)), 0.0)
    each_slab(turn)

    wrap(cell_b)
    operate(cell_b, cell_v)
    for s in range(2):
        for side, slab in sides_of_slab:
            send_rows[0, side, s] = packed(cell_b, s, side, slab)
            send_rows[1, side, s] = packed(cell_v, s, side, slab)
        send_columns(0, s, columns(cell_b, s) + columns(cell_v, s))
    pl.semaphore_wait(barrier, len(peers))
    start(col_copies(0))
    send_row_strips(0)
    send_row_strips(1)
    gram_s = gram(cell_b, halves_b)
    arrive(col_copies(0))
    send_relays()
    for s in range(2):
        for k in range(2):
            take_columns(cell_v, s, k, column_of(0, s, k, 0))
    hand_on(0)
    arrive(straight_copies(0) + hand_waits(0))
    for s in range(2):
        for side, slab in sides_of_slab:
            take_rows(cell_v, s, side, slab, recv_rows[0][row_at[s][side]].astype(F32))
    hand_on(1)
    wrap(cell_v)
    operate(cell_v, cell_q)
    arrive(straight_copies(1) + hand_waits(1))
    for s in range(2):
        for side, slab in sides_of_slab:
            take_rows(cell_q, s, side, slab, recv_rows[1][row_at[s][side]].astype(F32), cell_b)
        for k in range(2):
            back = jnp.concatenate(columns(cell_b, s)[8 * k:8 * k + 8], axis=0)
            take_columns(cell_q, s, k, column_of(0, s, k, 16) - back)
    arrive(relay_copies())
    take_corners(cell_q)
    for s in range(2):
        for side, slab in sides_of_slab:
            send_rows[2, side, s] = packed(cell_q, s, side, slab)
    send_row_strips(2)
    for s in range(2):
        send_columns(1, s, columns(cell_q, s))
    start(col_copies(1))
    gram_g = gram(cell_v, halves)

    gram_h = gram(cell_q, halves_q)
    own_a = jnp.concatenate([press(gram_s), press(gram_g), press(gram_h)], axis=0)
    part_a[...] = own_a
    plane_copies_a = exchange(in_plane, part_a, plane_a, 0)
    start(plane_copies_a)
    wrap(cell_q)
    operate(cell_q, cell_v)
    arrive(col_copies(1))
    for s in range(2):
        for k in range(2):
            take_columns(cell_v, s, k, column_of(1, s, k, 0))
    own_a = collect(plane_copies_a, own_a, plane_a)
    mid_a[...] = own_a
    depth_copies_a = exchange(along_z, mid_a, depth_a, 1)
    start(depth_copies_a)

    def inside(i, carry):
        halve(cell_v, halves, i // 6, i % 6 + 1)
        return carry
    lax.fori_loop(0, 12, inside, 0)
    gram_y = multiply(halves, 1, 7)
    hand_on(2)
    arrive(straight_copies(2) + hand_waits(2))
    for s in range(2):
        for side, slab in sides_of_slab:
            take_rows(cell_v, s, side, slab, recv_rows[2][row_at[s][side]].astype(F32))
    for s in range(2):
        for y in (0, 7):
            halve(cell_v, halves, s, y)
    own_b = press(fold(gram_y + multiply(halves, 0, 1) + multiply(halves, 7, 8)))
    part_b[...] = own_b
    plane_copies_b = exchange(in_plane, part_b, plane_b, 2)
    start(plane_copies_b)
    own_a = collect(depth_copies_a, own_a, depth_a)
    own_b = collect(plane_copies_b, own_b, plane_b)
    mid_b[...] = own_b
    depth_copies_b = exchange(along_z, mid_b, depth_b, 3)
    start(depth_copies_b)

    def symmetric(total, count):
        turned = jnp.transpose(jnp.concatenate([total, jnp.zeros((96, 128), F32)], axis=0))
        return [
            jnp.where(lane32 < 32, 0.5 * (roll(total, -32 * m) + turned[32 * m:32 * m + 32]), 0.0) for m in range(count)
        ]

    row_id = lax.broadcasted_iota(jnp.int32, (64, 128), 0)

    def eliminate(system, first):
        for base in range(first, first + 32, 8):
            spreads = [jnp.broadcast_to(system[:, base + j:base + j + 1], (64, 128)) for j in range(8)]
            for j in range(8):
                k, column = base + j, spreads[j]
                scale = 1.0 / column[k:k + 1, :]
                pivot = system[k:k + 1, :] * scale
                system = jnp.where(row_id == k, pivot, system - column * pivot)
                for m in range(j + 1, 8):
                    other = spreads[m][k:k + 1, :] * scale
                    spreads[m] = jnp.where(row_id == k, other, spreads[m] - column * other)
        return system

    s_mat, g_mat, h_mat = symmetric(sum(roll(spread(own_a[8 * m:8 * m + 8]), 32 * m) for m in range(3)), 3)
    system = jnp.concatenate([
        g_mat + roll(h_mat, 32) + roll(s_mat, 64),
        h_mat + roll(g_mat, 64),
    ], axis=0)
    system = eliminate(system, 0)
    own_b = collect(depth_copies_b, own_b, depth_b)
    (y_mat,) = symmetric(spread(own_b), 1)
    system = jnp.concatenate([system[0:32], system[32:64] + roll(y_mat, 32)], axis=0)
    system = eliminate(system, 32)
    mix = roll(jnp.where((lanes(64) >> 5) == 2, system, 0.0), 64)
    mix = mix + roll(mix, 32) + roll(mix, 64) + roll(mix, 96)
    pieces = [jnp.where((lane32 >> 5) == k, mix[32 * m:32 * m + 32], 0.0) for m in range(2) for k in range(4)]
    weights = jnp.concatenate([
        jnp.transpose(jnp.concatenate(pieces[0:4], axis=0)),
        jnp.transpose(jnp.concatenate(pieces[4:8], axis=0)),
    ], axis=1)
    weight_high, weight_low = split(weights)
    weight_both = jnp.concatenate([weight_high, weight_low], axis=0)
    across = (((1,), (1,)), ((), ()))

    def finish(s, y):
        row = pl.ds(pl.multiple_of(y * 128, 128), 128)
        high = jnp.concatenate([halves_b[s, row, 0:128], halves_q[s, row, 0:128]], axis=1)
        low = jnp.concatenate([halves_b[s, row, 128:256], halves_q[s, row, 128:256]], axis=1)
        first = lax.dot_general(weight_both, high, across, preferred_element_type=F32)
        second = lax.dot_general(weight_high, low, across, preferred_element_type=F32)
        value = first[0:128] + first[128:256] + second
        for k in range(4):
            result[pl.ds(s * 1024 + k * 8 + y, 32, stride=32), :] = value[32 * k:32 * k + 32]
    each_slab(finish, 4)
    for kind in range(3):
        for copy in straight_copies(kind) + cross_copies(kind) + hand_copies(kind):
            copy.wait_send()
    for copy in col_copies(0) + relay_copies() + col_copies(1):
        copy.wait_send()
    for copy in plane_copies_a + depth_copies_a + plane_copies_b + depth_copies_b:
        copy.wait_send()


def on_device(click_field, roughness, slot_block, neighbours, density, class_kappa):
    hbm = pl.BlockSpec(memory_space=pltpu.HBM)
    vmem = pl.BlockSpec(memory_space=pltpu.VMEM)
    dma = pltpu.SemaphoreType.DMA
    answer = pl.pallas_call(
        kernel,
        out_shape=jax.ShapeDtypeStruct((2048, 128), F32),
        in_specs=[hbm] * 6,
        out_specs=vmem,
        scratch_shapes=[
            pltpu.SMEM((128,), jnp.int32),
            pltpu.SMEM((4, 64), jnp.int32),
            pltpu.SMEM((64,), jnp.int32),
            pltpu.SMEM((4,), F32),
            pltpu.VMEM((64, 128), F32),
            pltpu.VMEM((2048, 128), F32),
            pltpu.VMEM((2, 10, 144, 128), F32),
            pltpu.VMEM((2, 10, 144, 128), F32),
            pltpu.VMEM((2, 10, 144, 128), F32),
            pltpu.VMEM((2, 8, 128, 128), F32),
            pltpu.VMEM((2, 1024, 256), BF16),
            pltpu.VMEM((2, 1024, 256), BF16),
            pltpu.VMEM((2, 1024, 256), BF16),
            pltpu.VMEM((3, 2, 2, 32, 128), BF16),
            pltpu.VMEM((2, 32, 128), BF16),
            pltpu.VMEM((2, 16, 128), BF16),
            *[pltpu.VMEM((10, 32, 128), BF16) for _ in range(3)],
            pltpu.VMEM((8, 2, 32, 128), BF16),
            pltpu.VMEM((8, 2, 16, 128), BF16),
            pltpu.VMEM((2, 8, 128), F32),
            pltpu.VMEM((5, 8, 128), F32),
            pltpu.VMEM((24, 128), F32), pltpu.VMEM((8, 24, 128), F32),
            pltpu.VMEM((24, 128), F32), pltpu.VMEM((8, 24, 128), F32),
            pltpu.VMEM((8, 128), F32), pltpu.VMEM((8, 8, 128), F32),
            pltpu.VMEM((8, 128), F32), pltpu.VMEM((8, 8, 128), F32),
            dma((5,)), dma((2,)),
            dma((3, 5)), dma((3, 5)),
            dma((2, 8)), dma((2, 8)),
            dma((5,)), dma((5,)),
            dma((4, 8)), dma((4, 8)),
        ],
        compiler_params=pltpu.CompilerParams(
            collective_id=0, has_side_effects=True, vmem_limit_bytes=60 * 1024 * 1024),
        name="smooth",
    )(
        slot_block, neighbours.T, density, class_kappa,
        click_field.reshape(2048, 128), roughness.reshape(64, 128),
    )
    return answer.reshape(click_field.shape)


def solution(mesh):
    return jax.shard_map(
        on_device,
        mesh=mesh,
        in_specs=(
            P(("region", "blk"), None, None, None),
            P(("region", "blk"), None, None),
            P("region"),
            P("region", None),
            P("region"),
            P(),
        ),
        out_specs=P(("region", "blk"), None, None, None),
        check_vma=False,
    )
```

```python
import jax
import jax.numpy as jnp
from jax import lax
from jax.experimental import pallas as pl
from jax.experimental.pallas import tpu as pltpu
from jax.sharding import PartitionSpec as P

F32, BF16 = jnp.float32, jnp.bfloat16
MESH = pl.DeviceIdType.MESH


def lanes(rows):
    return lax.broadcasted_iota(jnp.int32, (rows, 128), 1)


def roll(value, shift):
    return value if shift % 128 == 0 else pltpu.roll(value, shift % 128, 1)


def split(value):
    high = value.astype(BF16)
    low = (value - high.astype(F32)).astype(BF16)
    return high, low


def kernel(
    slots_in, near_in, density_in, kappas_in, field, rough_in, result,
    slots, near, density, kappas, rough,
    staged, cell_b, cell_v, cell_q, diag, halves_b, halves_q, halves,
    send_rows, send_cols_0, send_cols_1, rows_b, rows_v, rows_q, cols_0, cols_1, send_relay, relays,
    part_a, plane_a, mid_a, depth_a, part_b, plane_b, mid_b, depth_b,
    table_sem, in_sem, row_send, row_recv, col_send, col_recv, relay_send, relay_recv, sum_send, sum_recv,
):
    send_cols, recv_cols = (send_cols_0, send_cols_1), (cols_0, cols_1)
    recv_rows = (rows_b, rows_v, rows_q)
    region, me = lax.axis_index("region"), lax.axis_index("blk")
    depth, spot = me // 8, me % 8
    half, inner = spot // 4, spot % 4
    low_half = depth < 4
    straight = lax.rem(me + 32, 64)
    crossing = jnp.where(depth == 0, 7, jnp.where(depth == 7, 0, jnp.where(low_half, depth + 3, depth - 3)))

    def device(number):
        return (region, number)

    def in_plane(step):
        return depth * 8 + lax.rem(spot + step, 8)

    def in_crossing(step):
        return crossing * 8 + half * 4 + lax.rem(inner + step, 4)

    def along_z(step):
        return lax.rem(depth + step, 8) * 8 + spot

    barrier = pltpu.get_barrier_semaphore()
    peers = [in_plane(k) for k in range(1, 8)] + [along_z(k) for k in range(1, 8)] + [in_crossing(k) for k in range(1, 4)]
    for peer in peers:
        pl.semaphore_signal(barrier, inc=1, device_id=device(peer), device_id_type=MESH)

    tables = [
        pltpu.make_async_copy(source, target, table_sem.at[i])
        for i, (source, target) in enumerate((
            (slots_in, slots), (near_in, near), (density_in, density), (kappas_in, kappas), (rough_in, rough)))
    ]
    for copy in tables:
        copy.start()
    load = [pltpu.make_async_copy(field.at[pl.ds(s * 1024, 1024)], staged.at[pl.ds(s * 1024, 1024)], in_sem.at[s]) for s in range(2)]
    for copy in load:
        copy.start()

    for copy in tables:
        copy.wait()
    blocks = [slots[me * 2 + s] for s in range(2)]
    filled = [b >= 0 for b in blocks]
    safe = [jnp.maximum(b, 0) for b in blocks]
    kappa = [kappas[density[b]] for b in safe]
    sides = [[jnp.where(filled[s], near[k, safe[s]], -1) for k in range(4)] for s in range(2)]
    plane_ids = [slots[depth * 16 + u] for u in range(16)]
    cross_ids = [slots[(crossing * 2 + half) * 8 + u] for u in range(8)]
    straight_ids = [slots[straight * 2 + u] for u in range(2)]

    def find(block, ids):
        place = jnp.int32(0)
        for u, candidate in enumerate(ids):
            place = jnp.where(candidate == block, u, place)
        return place

    def look(side, block):
        return jnp.where(block >= 0, near[side, jnp.maximum(block, 0)], -1)

    def first_of(*choices):
        answer = choices[-1]
        for choice in choices[-2::-1]:
            answer = jnp.where(choice >= 0, choice, answer)
        return answer

    def plane_place(block):
        u = find(block, plane_ids)
        return (spot - (u >> 1)) & 7, u & 1

    col_at, row_at, flank_at, relay_at, corner = [], [], [], [], []
    for s in range(2):
        here, north, south = blocks[s], sides[s][2], sides[s][3]
        col_at.append([plane_place(sides[s][k]) for k in range(2)])
        flank_at.append([
            plane_place(first_of(sides[s][k], look(3, look(k, north)), look(2, look(k, south)))) for k in range(2)
        ])
        far = jnp.where(low_half, north, south)
        close = jnp.where(low_half, south, north)
        u, v = find(far, cross_ids), find(close, straight_ids)
        far_step, far_slot = (inner - (u >> 1)) & 3, u & 1
        spots = (u, 8 + v)
        places = ((far_step, far_slot), (jnp.int32(4), v))
        row_at.append((jnp.where(low_half, spots[0], spots[1]), jnp.where(low_half, spots[1], spots[0])))
        relay_at.append([
            tuple(jnp.where(low_half, places[side][i], places[1 - side][i]) for i in range(2)) for side in range(2)
        ])
        corner.append([[
            jnp.where(beyond >= 0, jnp.where(look(k, beyond) >= 0, 1.0, 0.0) + jnp.where(sides[s][k] >= 0, 1.0, 0.0), 0.0)
            for k in range(2)] for beyond in (north, south)])

    crossing_side = jnp.where(low_half, 0, 1)

    core, chip = inner % 2, inner // 2
    sibling = in_plane(1 - 2 * core + 8)

    def remote(source, target, send, recv, number):
        return pltpu.make_async_remote_copy(source, target, send, recv, device_id=device(number), device_id_type=MESH)

    def cross_copies(kind):
        source = send_rows.at[kind, crossing_side]
        target = recv_rows[kind].at[pl.ds(2 * inner, 2)]
        return [
            remote(source, target, row_send.at[kind, k], row_recv.at[kind, chip],
                   crossing * 8 + half * 4 + 2 * k + core)
            for k in range(2)
        ]

    def cross_waits(kind):
        return [
            remote(send_rows.at[kind, crossing_side], recv_rows[kind].at[pl.ds(2 * (2 * k + core), 2)],
                   row_send.at[kind, k], row_recv.at[kind, k], sibling)
            for k in range(2)
        ]

    def straight_copies(kind):
        return [remote(send_rows.at[kind, 1 - crossing_side], recv_rows[kind].at[pl.ds(8, 2)],
                       row_send.at[kind, 2], row_recv.at[kind, 2], straight)]

    def hand_copies(kind):
        return [
            remote(recv_rows[kind].at[pl.ds(2 * (2 * k + core), 2)], recv_rows[kind].at[pl.ds(2 * (2 * k + core), 2)],
                   row_send.at[kind, 3 + k], row_recv.at[kind, 3 + k], sibling)
            for k in range(2)
        ]

    def hand_waits(kind):
        return [
            remote(recv_rows[kind].at[pl.ds(2 * (2 * k + core), 2)], recv_rows[kind].at[pl.ds(2 * (2 * k + 1 - core), 2)],
                   row_send.at[kind, 3 + k], row_recv.at[kind, 3 + k], sibling)
            for k in range(2)
        ]

    def send_row_strips(kind):
        start(straight_copies(kind) + cross_copies(kind))

    def hand_on(kind):
        arrive(cross_waits(kind))
        start(hand_copies(kind))

    def relay_copies():
        return [
            remote(send_relay.at[crossing_side], relays.at[k], relay_send.at[k], relay_recv.at[k], in_crossing(k))
            for k in range(4)
        ] + [remote(send_relay.at[1 - crossing_side], relays.at[4], relay_send.at[4], relay_recv.at[4], straight)]

    def col_copies(level):
        return [
            pltpu.make_async_remote_copy(
                send_cols[level], recv_cols[level].at[k],
                col_send.at[level, k], col_recv.at[level, k],
                device_id=device(in_plane(k)), device_id_type=MESH)
            for k in range(1, 8)
        ]

    lane32, lane128 = lanes(32), lanes(128)

    sides_of_slab = ((0, 1), (1, 8))

    def packed(cells, s, side, slab):
        answer = jnp.zeros((32, 128), F32)
        for k in range(4):
            piece = roll(cells[s, slab, 8 + 32 * k:40 + 32 * k, :], 32 * k - 96 * side)
            answer = jnp.where((lane32 >> 5) == k, piece, answer)
        return answer.astype(BF16)

    def columns(cells, s):
        return [cells[s, 1 + y, row:row + 1, :] for row in (8, 135) for y in range(8)]

    def send_columns(level, s, rows):
        strip = jnp.concatenate(rows, axis=0).astype(BF16)
        send_cols[level][s] = strip
        recv_cols[level][0, s] = strip

    def start(copies):
        for copy in copies:
            copy.start()

    def arrive(copies):
        for copy in copies:
            copy.wait_recv()

    def linked(s, k):
        return sides[s][k] >= 0

    def column_of(level, s, k, first):
        step, slot = col_at[s][k]
        strip = recv_cols[level][step, slot].astype(F32)
        return strip[first + 8:first + 16] if k == 0 else strip[first:first + 8]

    def take_columns(cells, s, k, strip):
        row = (8, 135)[k]
        strip = jnp.where(linked(s, k), strip, 0.0)
        for y in range(8):
            cells[s, 1 + y, row:row + 1, :] = cells[s, 1 + y, row:row + 1, :] - strip[y:y + 1]

    def take_rows(cells, s, side, slab, strip, back=None):
        touching = (lane32 >> 5) == 3 * side
        for k in range(4):
            rows = slice(8 + 32 * k, 40 + 32 * k)
            piece = roll(strip, 96 * side - 32 * k)
            if back is not None:
                piece = piece - back[s, slab, rows, :]
            piece = jnp.where(touching, jnp.where(linked(s, 2 + side), piece, 0.0), 0.0)
            cells[s, slab, rows, :] = cells[s, slab, rows, :] - piece

    def send_relays():
        top = lax.broadcasted_iota(jnp.int32, (8, 128), 0)
        lane8 = lanes(8)
        found = []
        for s in range(2):
            (west_step, west_slot), (east_step, east_slot) = flank_at[s]
            found.append((
                recv_cols[0][west_step, west_slot].astype(F32)[8:16],
                recv_cols[0][east_step, east_slot].astype(F32)[0:8],
            ))
        for side in range(2):
            lines = []
            for west, east in found:
                row = slice(7 * side, 7 * side + 1)
                line = jnp.where(lanes(1) < 32, roll(west[row], 32 * side), roll(east[row], 32 + 32 * side))
                lines.append(jnp.broadcast_to(line, (8, 128)))
            value = jnp.where(top == 0, lines[0], lines[1])
            send_relay[side] = jnp.where(lane8 < 64, value, 0.0)
        start(relay_copies())

    def take_corners(cells):
        for s in range(2):
            for side, slab in sides_of_slab:
                index, slot = relay_at[s][side]
                tile = relays[index]
                line = jnp.where(slot == 0, tile[0:1], tile[1:2])
                for k, row in ((0, 8), (1, 135)):
                    factor = corner[s][side][k]
                    value = jnp.where(factor > 0.0, roll(line, 96 * side - 32 * k) * factor, 0.0)
                    value = jnp.where((lanes(1) >> 5) == 3 * side, value, 0.0)
                    cells[s, slab, row:row + 1, :] = cells[s, slab, row:row + 1, :] + value

    def wrap(cells):
        for s in range(2):
            cells[s, 0, 8:136, :] = jnp.where(lane128 < 32, 0.0, roll(cells[s, 8, 8:136, :], 32))
            cells[s, 9, 8:136, :] = jnp.where(lane128 >= 96, 0.0, roll(cells[s, 1, 8:136, :], 96))

    def each_slab(body, unroll=2):
        def step(i, carry):
            body(i >> 3, i & 7)
            return carry
        lax.fori_loop(0, 16, step, 0, unroll=unroll)

    def operate(source, target):
        def body(s, y):
            centre = source[s, y + 1, 8:136, :]
            beside = source[s, y + 1, 7:135, :] + source[s, y + 1, 9:137, :]
            along = source[s, y, 8:136, :] + source[s, y + 2, 8:136, :]
            target[s, y + 1, 8:136, :] = diag[s, y] * centre - (beside + along)
        each_slab(body)

    def multiply(parts, first, last):
        total = jnp.zeros((128, 256), F32)
        for s in range(2):
            rows = slice(first * 128, last * 128)
            total = total + lax.dot_general(
                parts[s, rows, 0:128], parts[s, rows, :], (((0,), (0,)), ((), ())), preferred_element_type=F32)
        return total

    def halve(cells, parts, s, y):
        high, low = split(cells[s, y + 1, 8:136, :])
        row = pl.ds(pl.multiple_of(y * 128, 128), 128)
        parts[s, row, 0:128] = high
        parts[s, row, 128:256] = low

    def fold(total):
        total = total[:, 0:128] + 2.0 * total[:, 128:256]
        answer = total[0:32]
        for k in range(1, 4):
            answer = answer + roll(total[32 * k:32 * k + 32], -32 * k)
        return jnp.where(lane32 < 32, answer, 0.0)

    def gram(cells, parts):
        each_slab(lambda s, y: halve(cells, parts, s, y))
        return fold(multiply(parts, 0, 8))

    def press(value):
        answer = value[0:8]
        for k in range(1, 4):
            answer = answer + roll(value[8 * k:8 * k + 8], 32 * k)
        return answer

    def spread(value):
        return jnp.concatenate([jnp.where(lanes(8) < 32, roll(value, -32 * k), 0.0) for k in range(4)], axis=0)

    def exchange(peer, source, target, index):
        return [
            pltpu.make_async_remote_copy(
                source, target.at[k], sum_send.at[index, k], sum_recv.at[index, k],
                device_id=device(peer(k)), device_id_type=MESH)
            for k in range(1, 8)
        ]

    def collect(copies, own, target):
        for k, copy in enumerate(copies):
            copy.wait_recv()
            own = own + target[k + 1]
        return own

    blank = jnp.zeros((8, 128), F32)
    for cells in (cell_b, cell_v, cell_q):
        for s in range(2):
            for y in range(10):
                cells[s, y, 0:8, :] = blank
                cells[s, y, 136:144, :] = blank

    def fill_diag(s, y):
        value = jnp.where(s == 0, kappa[0], kappa[1])
        rows = [jnp.broadcast_to(rough[pl.ds(s * 32 + k * 8 + y, 1), :], (32, 128)) for k in range(4)]
        diag[s, y] = jnp.transpose(jnp.concatenate(rows, axis=0)) * value + 4.0
    each_slab(fill_diag)

    for copy in load:
        copy.wait()

    def turn(s, y):
        keep = jnp.where(s == 0, blocks[0], blocks[1]) >= 0
        rows = [staged[pl.ds(s * 1024 + k * 8 + y, 32, stride=32), :] for k in range(4)]
        cell_b[s, y + 1, 8:136, :] = jnp.where(keep, jnp.transpose(jnp.concatenate(rows, axis=0)), 0.0)
    each_slab(turn)

    wrap(cell_b)
    operate(cell_b, cell_v)
    for s in range(2):
        for side, slab in sides_of_slab:
            send_rows[0, side, s] = packed(cell_b, s, side, slab)
            send_rows[1, side, s] = packed(cell_v, s, side, slab)
        send_columns(0, s, columns(cell_b, s) + columns(cell_v, s))
    pl.semaphore_wait(barrier, len(peers))
    start(col_copies(0))
    send_row_strips(0)
    send_row_strips(1)
    gram_s = gram(cell_b, halves_b)
    arrive(col_copies(0))
    send_relays()
    for s in range(2):
        for k in range(2):
            take_columns(cell_v, s, k, column_of(0, s, k, 0))
    hand_on(0)
    arrive(straight_copies(0) + hand_waits(0))
    for s in range(2):
        for side, slab in sides_of_slab:
            take_rows(cell_v, s, side, slab, recv_rows[0][row_at[s][side]].astype(F32))
    hand_on(1)
    wrap(cell_v)
    operate(cell_v, cell_q)
    arrive(straight_copies(1) + hand_waits(1))
    for s in range(2):
        for side, slab in sides_of_slab:
            take_rows(cell_q, s, side, slab, recv_rows[1][row_at[s][side]].astype(F32), cell_b)
        for k in range(2):
            back = jnp.concatenate(columns(cell_b, s)[8 * k:8 * k + 8], axis=0)
            take_columns(cell_q, s, k, column_of(0, s, k, 16) - back)
    arrive(relay_copies())
    take_corners(cell_q)
    for s in range(2):
        for side, slab in sides_of_slab:
            send_rows[2, side, s] = packed(cell_q, s, side, slab)
    send_row_strips(2)
    for s in range(2):
        send_columns(1, s, columns(cell_q, s))
    start(col_copies(1))
    gram_g = gram(cell_v, halves)

    gram_h = gram(cell_q, halves_q)
    own_a = jnp.concatenate([press(gram_s), press(gram_g), press(gram_h)], axis=0)
    part_a[...] = own_a
    plane_copies_a = exchange(in_plane, part_a, plane_a, 0)
    start(plane_copies_a)
    wrap(cell_q)
    operate(cell_q, cell_v)
    arrive(col_copies(1))
    for s in range(2):
        for k in range(2):
            take_columns(cell_v, s, k, column_of(1, s, k, 0))
    own_a = collect(plane_copies_a, own_a, plane_a)
    mid_a[...] = own_a
    depth_copies_a = exchange(along_z, mid_a, depth_a, 1)
    start(depth_copies_a)

    def inside(i, carry):
        halve(cell_v, halves, i // 6, i % 6 + 1)
        return carry
    lax.fori_loop(0, 12, inside, 0)
    gram_y = multiply(halves, 1, 7)
    hand_on(2)
    arrive(straight_copies(2) + hand_waits(2))
    for s in range(2):
        for side, slab in sides_of_slab:
            take_rows(cell_v, s, side, slab, recv_rows[2][row_at[s][side]].astype(F32))
    for s in range(2):
        for y in (0, 7):
            halve(cell_v, halves, s, y)
    own_b = press(fold(gram_y + multiply(halves, 0, 1) + multiply(halves, 7, 8)))
    part_b[...] = own_b
    plane_copies_b = exchange(in_plane, part_b, plane_b, 2)
    start(plane_copies_b)
    own_b = collect(plane_copies_b, own_b, plane_b)
    mid_b[...] = own_b
    depth_copies_b = exchange(along_z, mid_b, depth_b, 3)
    start(depth_copies_b)

    def symmetric(total, count):
        turned = jnp.transpose(jnp.concatenate([total, jnp.zeros((96, 128), F32)], axis=0))
        return [
            jnp.where(lane32 < 32, 0.5 * (roll(total, -32 * m) + turned[32 * m:32 * m + 32]), 0.0) for m in range(count)
        ]

    row_id = lax.broadcasted_iota(jnp.int32, (64, 128), 0)

    def eliminate(system, first):
        for base in range(first, first + 32, 8):
            spreads = [jnp.broadcast_to(system[:, base + j:base + j + 1], (64, 128)) for j in range(8)]
            for j in range(8):
                k, column = base + j, spreads[j]
                scale = 1.0 / column[k:k + 1, :]
                pivot = system[k:k + 1, :] * scale
                system = jnp.where(row_id == k, pivot, system - column * pivot)
                for m in range(j + 1, 8):
                    other = spreads[m][k:k + 1, :] * scale
                    spreads[m] = jnp.where(row_id == k, other, spreads[m] - column * other)
        return system

    own_a = collect(depth_copies_a, own_a, depth_a)
    s_mat, g_mat, h_mat = symmetric(sum(roll(spread(own_a[8 * m:8 * m + 8]), 32 * m) for m in range(3)), 3)
    system = jnp.concatenate([
        g_mat + roll(h_mat, 32) + roll(s_mat, 64),
        h_mat + roll(g_mat, 64),
    ], axis=0)
    system = eliminate(system, 0)
    own_b = collect(depth_copies_b, own_b, depth_b)
    (y_mat,) = symmetric(spread(own_b), 1)
    system = jnp.concatenate([system[0:32], system[32:64] + roll(y_mat, 32)], axis=0)
    system = eliminate(system, 32)
    mix = roll(jnp.where((lanes(64) >> 5) == 2, system, 0.0), 64)
    mix = mix + roll(mix, 32) + roll(mix, 64) + roll(mix, 96)
    pieces = [jnp.where((lane32 >> 5) == k, mix[32 * m:32 * m + 32], 0.0) for m in range(2) for k in range(4)]
    weights = jnp.concatenate([
        jnp.transpose(jnp.concatenate(pieces[0:4], axis=0)),
        jnp.transpose(jnp.concatenate(pieces[4:8], axis=0)),
    ], axis=1)
    weight_high, weight_low = split(weights)
    weight_both = jnp.concatenate([weight_high, weight_low], axis=0)
    across = (((1,), (1,)), ((), ()))

    def finish(s, y):
        row = pl.ds(pl.multiple_of(y * 128, 128), 128)
        high = jnp.concatenate([halves_b[s, row, 0:128], halves_q[s, row, 0:128]], axis=1)
        low = jnp.concatenate([halves_b[s, row, 128:256], halves_q[s, row, 128:256]], axis=1)
        first = lax.dot_general(weight_both, high, across, preferred_element_type=F32)
        second = lax.dot_general(weight_high, low, across, preferred_element_type=F32)
        value = first[0:128] + first[128:256] + second
        for k in range(4):
            result[pl.ds(s * 1024 + k * 8 + y, 32, stride=32), :] = value[32 * k:32 * k + 32]
    each_slab(finish, 16)
    for kind in range(3):
        for copy in straight_copies(kind) + cross_copies(kind) + hand_copies(kind):
            copy.wait_send()
    for copy in col_copies(0) + relay_copies() + col_copies(1):
        copy.wait_send()
    for copy in plane_copies_a + depth_copies_a + plane_copies_b + depth_copies_b:
        copy.wait_send()


def on_device(click_field, roughness, slot_block, neighbours, density, class_kappa):
    hbm = pl.BlockSpec(memory_space=pltpu.HBM)
    vmem = pl.BlockSpec(memory_space=pltpu.VMEM)
    dma = pltpu.SemaphoreType.DMA
    answer = pl.pallas_call(
        kernel,
        out_shape=jax.ShapeDtypeStruct((2048, 128), F32),
        in_specs=[hbm] * 6,
        out_specs=vmem,
        scratch_shapes=[
            pltpu.SMEM((128,), jnp.int32),
            pltpu.SMEM((4, 64), jnp.int32),
            pltpu.SMEM((64,), jnp.int32),
            pltpu.SMEM((4,), F32),
            pltpu.VMEM((64, 128), F32),
            pltpu.VMEM((2048, 128), F32),
            pltpu.VMEM((2, 10, 144, 128), F32),
            pltpu.VMEM((2, 10, 144, 128), F32),
            pltpu.VMEM((2, 10, 144, 128), F32),
            pltpu.VMEM((2, 8, 128, 128), F32),
            pltpu.VMEM((2, 1024, 256), BF16),
            pltpu.VMEM((2, 1024, 256), BF16),
            pltpu.VMEM((2, 1024, 256), BF16),
            pltpu.VMEM((3, 2, 2, 32, 128), BF16),
            pltpu.VMEM((2, 32, 128), BF16),
            pltpu.VMEM((2, 16, 128), BF16),
            *[pltpu.VMEM((10, 32, 128), BF16) for _ in range(3)],
            pltpu.VMEM((8, 2, 32, 128), BF16),
            pltpu.VMEM((8, 2, 16, 128), BF16),
            pltpu.VMEM((2, 8, 128), F32),
            pltpu.VMEM((5, 8, 128), F32),
            pltpu.VMEM((24, 128), F32), pltpu.VMEM((8, 24, 128), F32),
            pltpu.VMEM((24, 128), F32), pltpu.VMEM((8, 24, 128), F32),
            pltpu.VMEM((8, 128), F32), pltpu.VMEM((8, 8, 128), F32),
            pltpu.VMEM((8, 128), F32), pltpu.VMEM((8, 8, 128), F32),
            dma((5,)), dma((2,)),
            dma((3, 5)), dma((3, 5)),
            dma((2, 8)), dma((2, 8)),
            dma((5,)), dma((5,)),
            dma((4, 8)), dma((4, 8)),
        ],
        compiler_params=pltpu.CompilerParams(
            collective_id=0, has_side_effects=True, vmem_limit_bytes=40 * 1024 * 1024),
        name="smooth",
    )(
        *[pltpu.with_memory_space_constraint(x, pltpu.HBM) for x in (
            slot_block, neighbours.T, density, class_kappa,
            click_field.reshape(2048, 128), roughness.reshape(64, 128))]
    )
    return answer.reshape(click_field.shape)


def solution(mesh):
    return jax.shard_map(
        on_device,
        mesh=mesh,
        in_specs=(
            P(("region", "blk"), None, None, None),
            P(("region", "blk"), None, None),
            P("region"),
            P("region", None),
            P("region"),
            P(),
        ),
        out_specs=P(("region", "blk"), None, None, None),
        check_vma=False,
    )
```

```python
import jax
import jax.numpy as jnp
from jax import lax
from jax.experimental import pallas as pl
from jax.experimental.pallas import tpu as pltpu
from jax.sharding import PartitionSpec as P

F32, BF16 = jnp.float32, jnp.bfloat16
MESH = pl.DeviceIdType.MESH


def lanes(rows):
    return lax.broadcasted_iota(jnp.int32, (rows, 128), 1)


def roll(value, shift):
    return value if shift % 128 == 0 else pltpu.roll(value, shift % 128, 1)


def split(value):
    high = value.astype(BF16)
    low = (value - high.astype(F32)).astype(BF16)
    return high, low


def kernel(
    slots_in, near_in, density_in, kappas_in, field, rough_in, result,
    slots, near, density, kappas, rough,
    staged, cell_b, cell_v, cell_q, diag, halves_b, halves_q, halves,
    send_rows, send_cols_0, send_cols_1, rows_b, rows_v, rows_q, cols_0, cols_1, send_relay, relays,
    part_a, plane_a, mid_a, depth_a, part_b, plane_b, mid_b, depth_b,
    table_sem, in_sem, row_send, row_recv, col_send, col_recv, relay_send, relay_recv, sum_send, sum_recv,
):
    send_cols, recv_cols = (send_cols_0, send_cols_1), (cols_0, cols_1)
    recv_rows = (rows_b, rows_v, rows_q)
    region, me = lax.axis_index("region"), lax.axis_index("blk")
    depth, spot = me // 8, me % 8
    half, inner = spot // 4, spot % 4
    low_half = depth < 4
    straight = lax.rem(me + 32, 64)
    crossing = jnp.where(depth == 0, 7, jnp.where(depth == 7, 0, jnp.where(low_half, depth + 3, depth - 3)))

    def device(number):
        return (region, number)

    def in_plane(step):
        return depth * 8 + lax.rem(spot + step, 8)

    def in_crossing(step):
        return crossing * 8 + half * 4 + lax.rem(inner + step, 4)

    def along_z(step):
        return lax.rem(depth + step, 8) * 8 + spot

    barrier = pltpu.get_barrier_semaphore()
    peers = [in_plane(k) for k in range(1, 8)] + [along_z(k) for k in range(1, 8)] + [in_crossing(k) for k in range(1, 4)]
    for peer in peers:
        pl.semaphore_signal(barrier, inc=1, device_id=device(peer), device_id_type=MESH)

    tables = [
        pltpu.make_async_copy(source, target, table_sem.at[i])
        for i, (source, target) in enumerate((
            (slots_in, slots), (near_in, near), (density_in, density), (kappas_in, kappas), (rough_in, rough)))
    ]
    for copy in tables:
        copy.start()
    load = [pltpu.make_async_copy(field.at[pl.ds(s * 1024, 1024)], staged.at[pl.ds(s * 1024, 1024)], in_sem.at[s]) for s in range(2)]
    for copy in load:
        copy.start()

    for copy in tables:
        copy.wait()
    blocks = [slots[me * 2 + s] for s in range(2)]
    filled = [b >= 0 for b in blocks]
    safe = [jnp.maximum(b, 0) for b in blocks]
    kappa = [kappas[density[b]] for b in safe]
    sides = [[jnp.where(filled[s], near[k, safe[s]], -1) for k in range(4)] for s in range(2)]
    plane_ids = [slots[depth * 16 + u] for u in range(16)]
    cross_ids = [slots[(crossing * 2 + half) * 8 + u] for u in range(8)]
    straight_ids = [slots[straight * 2 + u] for u in range(2)]

    def find(block, ids):
        place = jnp.int32(0)
        for u, candidate in enumerate(ids):
            place = jnp.where(candidate == block, u, place)
        return place

    def look(side, block):
        return jnp.where(block >= 0, near[side, jnp.maximum(block, 0)], -1)

    def first_of(*choices):
        answer = choices[-1]
        for choice in choices[-2::-1]:
            answer = jnp.where(choice >= 0, choice, answer)
        return answer

    def plane_place(block):
        u = find(block, plane_ids)
        return (spot - (u >> 1)) & 7, u & 1

    col_at, row_at, flank_at, relay_at, corner = [], [], [], [], []
    for s in range(2):
        here, north, south = blocks[s], sides[s][2], sides[s][3]
        col_at.append([plane_place(sides[s][k]) for k in range(2)])
        flank_at.append([
            plane_place(first_of(sides[s][k], look(3, look(k, north)), look(2, look(k, south)))) for k in range(2)
        ])
        far = jnp.where(low_half, north, south)
        close = jnp.where(low_half, south, north)
        u, v = find(far, cross_ids), find(close, straight_ids)
        far_step, far_slot = (inner - (u >> 1)) & 3, u & 1
        spots = (u, 8 + v)
        places = ((far_step, far_slot), (jnp.int32(4), v))
        row_at.append((jnp.where(low_half, spots[0], spots[1]), jnp.where(low_half, spots[1], spots[0])))
        relay_at.append([
            tuple(jnp.where(low_half, places[side][i], places[1 - side][i]) for i in range(2)) for side in range(2)
        ])
        corner.append([[
            jnp.where(beyond >= 0, jnp.where(look(k, beyond) >= 0, 1.0, 0.0) + jnp.where(sides[s][k] >= 0, 1.0, 0.0), 0.0)
            for k in range(2)] for beyond in (north, south)])

    crossing_side = jnp.where(low_half, 0, 1)

    core, chip = inner % 2, inner // 2
    sibling = in_plane(1 - 2 * core + 8)

    def remote(source, target, send, recv, number):
        return pltpu.make_async_remote_copy(source, target, send, recv, device_id=device(number), device_id_type=MESH)

    def cross_copies(kind):
        source = send_rows.at[kind, crossing_side]
        target = recv_rows[kind].at[pl.ds(2 * inner, 2)]
        return [
            remote(source, target, row_send.at[kind, k], row_recv.at[kind, chip],
                   crossing * 8 + half * 4 + 2 * k + core)
            for k in range(2)
        ]

    def cross_waits(kind):
        return [
            remote(send_rows.at[kind, crossing_side], recv_rows[kind].at[pl.ds(2 * (2 * k + core), 2)],
                   row_send.at[kind, k], row_recv.at[kind, k], sibling)
            for k in range(2)
        ]

    def straight_copies(kind):
        return [remote(send_rows.at[kind, 1 - crossing_side], recv_rows[kind].at[pl.ds(8, 2)],
                       row_send.at[kind, 2], row_recv.at[kind, 2], straight)]

    def hand_copies(kind):
        return [
            remote(recv_rows[kind].at[pl.ds(2 * (2 * k + core), 2)], recv_rows[kind].at[pl.ds(2 * (2 * k + core), 2)],
                   row_send.at[kind, 3 + k], row_recv.at[kind, 3 + k], sibling)
            for k in range(2)
        ]

    def hand_waits(kind):
        return [
            remote(recv_rows[kind].at[pl.ds(2 * (2 * k + core), 2)], recv_rows[kind].at[pl.ds(2 * (2 * k + 1 - core), 2)],
                   row_send.at[kind, 3 + k], row_recv.at[kind, 3 + k], sibling)
            for k in range(2)
        ]

    def send_row_strips(kind):
        start(cross_copies(kind) + straight_copies(kind))

    def hand_on(kind):
        arrive(cross_waits(kind))
        start(hand_copies(kind))

    def relay_copies():
        return [
            remote(send_relay.at[crossing_side], relays.at[k], relay_send.at[k], relay_recv.at[k], in_crossing(k))
            for k in range(4)
        ] + [remote(send_relay.at[1 - crossing_side], relays.at[4], relay_send.at[4], relay_recv.at[4], straight)]

    def col_copies(level):
        return [
            pltpu.make_async_remote_copy(
                send_cols[level], recv_cols[level].at[k],
                col_send.at[level, k], col_recv.at[level, k],
                device_id=device(in_plane(k)), device_id_type=MESH)
            for k in range(1, 8)
        ]

    lane32, lane128 = lanes(32), lanes(128)

    sides_of_slab = ((0, 1), (1, 8))

    def packed(cells, s, side, slab):
        answer = jnp.zeros((32, 128), F32)
        for k in range(4):
            piece = roll(cells[s, slab, 8 + 32 * k:40 + 32 * k, :], 32 * k - 96 * side)
            answer = jnp.where((lane32 >> 5) == k, piece, answer)
        return answer.astype(BF16)

    def columns(cells, s):
        return [cells[s, 1 + y, row:row + 1, :] for row in (8, 135) for y in range(8)]

    def send_columns(level, s, rows):
        strip = jnp.concatenate(rows, axis=0).astype(BF16)
        send_cols[level][s] = strip
        recv_cols[level][0, s] = strip

    def start(copies):
        for copy in copies:
            copy.start()

    def arrive(copies):
        for copy in copies:
            copy.wait_recv()

    def linked(s, k):
        return sides[s][k] >= 0

    def column_of(level, s, k, first):
        step, slot = col_at[s][k]
        strip = recv_cols[level][step, slot].astype(F32)
        return strip[first + 8:first + 16] if k == 0 else strip[first:first + 8]

    def take_columns(cells, s, k, strip):
        row = (8, 135)[k]
        strip = jnp.where(linked(s, k), strip, 0.0)
        for y in range(8):
            cells[s, 1 + y, row:row + 1, :] = cells[s, 1 + y, row:row + 1, :] - strip[y:y + 1]

    def take_rows(cells, s, side, slab, strip, back=None):
        touching = (lane32 >> 5) == 3 * side
        for k in range(4):
            rows = slice(8 + 32 * k, 40 + 32 * k)
            piece = roll(strip, 96 * side - 32 * k)
            if back is not None:
                piece = piece - back[s, slab, rows, :]
            piece = jnp.where(touching, jnp.where(linked(s, 2 + side), piece, 0.0), 0.0)
            cells[s, slab, rows, :] = cells[s, slab, rows, :] - piece

    def send_relays():
        top = lax.broadcasted_iota(jnp.int32, (8, 128), 0)
        lane8 = lanes(8)
        found = []
        for s in range(2):
            (west_step, west_slot), (east_step, east_slot) = flank_at[s]
            found.append((
                recv_cols[0][west_step, west_slot].astype(F32)[8:16],
                recv_cols[0][east_step, east_slot].astype(F32)[0:8],
            ))
        for side in range(2):
            lines = []
            for west, east in found:
                row = slice(7 * side, 7 * side + 1)
                line = jnp.where(lanes(1) < 32, roll(west[row], 32 * side), roll(east[row], 32 + 32 * side))
                lines.append(jnp.broadcast_to(line, (8, 128)))
            value = jnp.where(top == 0, lines[0], lines[1])
            send_relay[side] = jnp.where(lane8 < 64, value, 0.0)
        start(relay_copies())

    def take_corners(cells):
        for s in range(2):
            for side, slab in sides_of_slab:
                index, slot = relay_at[s][side]
                tile = relays[index]
                line = jnp.where(slot == 0, tile[0:1], tile[1:2])
                for k, row in ((0, 8), (1, 135)):
                    factor = corner[s][side][k]
                    value = jnp.where(factor > 0.0, roll(line, 96 * side - 32 * k) * factor, 0.0)
                    value = jnp.where((lanes(1) >> 5) == 3 * side, value, 0.0)
                    cells[s, slab, row:row + 1, :] = cells[s, slab, row:row + 1, :] + value

    def wrap(cells):
        for s in range(2):
            cells[s, 0, 8:136, :] = jnp.where(lane128 < 32, 0.0, roll(cells[s, 8, 8:136, :], 32))
            cells[s, 9, 8:136, :] = jnp.where(lane128 >= 96, 0.0, roll(cells[s, 1, 8:136, :], 96))

    def each_slab(body, unroll=8):
        def step(i, carry):
            body(i >> 3, i & 7)
            return carry
        lax.fori_loop(0, 16, step, 0, unroll=unroll)

    def operate(source, target):
        def body(s, y):
            centre = source[s, y + 1, 8:136, :]
            beside = source[s, y + 1, 7:135, :] + source[s, y + 1, 9:137, :]
            along = source[s, y, 8:136, :] + source[s, y + 2, 8:136, :]
            target[s, y + 1, 8:136, :] = diag[s, y] * centre - (beside + along)
        each_slab(body)

    def multiply(parts, first, last):
        total = jnp.zeros((128, 256), F32)
        for s in range(2):
            rows = slice(first * 128, last * 128)
            total = total + lax.dot_general(
                parts[s, rows, 0:128], parts[s, rows, :], (((0,), (0,)), ((), ())), preferred_element_type=F32)
        return total

    def halve(cells, parts, s, y):
        high, low = split(cells[s, y + 1, 8:136, :])
        row = pl.ds(pl.multiple_of(y * 128, 128), 128)
        parts[s, row, 0:128] = high
        parts[s, row, 128:256] = low

    def fold(total):
        total = total[:, 0:128] + 2.0 * total[:, 128:256]
        answer = total[0:32]
        for k in range(1, 4):
            answer = answer + roll(total[32 * k:32 * k + 32], -32 * k)
        return jnp.where(lane32 < 32, answer, 0.0)

    def gram(cells, parts):
        each_slab(lambda s, y: halve(cells, parts, s, y))
        return fold(multiply(parts, 0, 8))

    def press(value):
        answer = value[0:8]
        for k in range(1, 4):
            answer = answer + roll(value[8 * k:8 * k + 8], 32 * k)
        return answer

    def spread(value):
        return jnp.concatenate([jnp.where(lanes(8) < 32, roll(value, -32 * k), 0.0) for k in range(4)], axis=0)

    def exchange(peer, source, target, index):
        return [
            pltpu.make_async_remote_copy(
                source, target.at[k], sum_send.at[index, k], sum_recv.at[index, k],
                device_id=device(peer(k)), device_id_type=MESH)
            for k in range(1, 8)
        ]

    def collect(copies, own, target):
        for k, copy in enumerate(copies):
            copy.wait_recv()
            own = own + target[k + 1]
        return own

    blank = jnp.zeros((8, 128), F32)
    for cells in (cell_b, cell_v, cell_q):
        for s in range(2):
            for y in range(10):
                cells[s, y, 0:8, :] = blank
                cells[s, y, 136:144, :] = blank

    def fill_diag(s, y):
        value = jnp.where(s == 0, kappa[0], kappa[1])
        rows = [jnp.broadcast_to(rough[pl.ds(s * 32 + k * 8 + y, 1), :], (32, 128)) for k in range(4)]
        diag[s, y] = jnp.transpose(jnp.concatenate(rows, axis=0)) * value + 4.0
    each_slab(fill_diag)

    for copy in load:
        copy.wait()

    def turn(s, y):
        keep = jnp.where(s == 0, blocks[0], blocks[1]) >= 0
        rows = [staged[pl.ds(s * 1024 + k * 8 + y, 32, stride=32), :] for k in range(4)]
        cell_b[s, y + 1, 8:136, :] = jnp.where(keep, jnp.transpose(jnp.concatenate(rows, axis=0)), 0.0)
    each_slab(turn)

    wrap(cell_b)
    operate(cell_b, cell_v)
    for s in range(2):
        for side, slab in sides_of_slab:
            send_rows[0, side, s] = packed(cell_b, s, side, slab)
            send_rows[1, side, s] = packed(cell_v, s, side, slab)
        send_columns(0, s, columns(cell_b, s) + columns(cell_v, s))
    pl.semaphore_wait(barrier, len(peers))
    start(cross_copies(0) + straight_copies(0) + col_copies(0) + cross_copies(1) + straight_copies(1))
    gram_s = gram(cell_b, halves_b)
    arrive(col_copies(0))
    send_relays()
    for s in range(2):
        for k in range(2):
            take_columns(cell_v, s, k, column_of(0, s, k, 0))
    hand_on(0)
    arrive(straight_copies(0) + hand_waits(0))
    for s in range(2):
        for side, slab in sides_of_slab:
            take_rows(cell_v, s, side, slab, recv_rows[0][row_at[s][side]].astype(F32))
    hand_on(1)
    wrap(cell_v)
    operate(cell_v, cell_q)
    for s in range(2):
        for k in range(2):
            back = jnp.concatenate(columns(cell_b, s)[8 * k:8 * k + 8], axis=0)
            take_columns(cell_q, s, k, column_of(0, s, k, 16) - back)
    arrive(relay_copies())
    take_corners(cell_q)
    arrive(straight_copies(1) + hand_waits(1))
    for s in range(2):
        for side, slab in sides_of_slab:
            take_rows(cell_q, s, side, slab, recv_rows[1][row_at[s][side]].astype(F32), cell_b)
    for s in range(2):
        for side, slab in sides_of_slab:
            send_rows[2, side, s] = packed(cell_q, s, side, slab)
    send_row_strips(2)
    for s in range(2):
        send_columns(1, s, columns(cell_q, s))
    start(col_copies(1))
    gram_g = gram(cell_v, halves)

    gram_h = gram(cell_q, halves_q)
    own_a = jnp.concatenate([press(gram_s), press(gram_g), press(gram_h)], axis=0)
    part_a[...] = own_a
    plane_copies_a = exchange(in_plane, part_a, plane_a, 0)
    start(plane_copies_a)
    wrap(cell_q)
    operate(cell_q, cell_v)
    arrive(col_copies(1))
    for s in range(2):
        for k in range(2):
            take_columns(cell_v, s, k, column_of(1, s, k, 0))
    own_a = collect(plane_copies_a, own_a, plane_a)
    mid_a[...] = own_a
    depth_copies_a = exchange(along_z, mid_a, depth_a, 1)
    start(depth_copies_a)

    def inside(i, carry):
        halve(cell_v, halves, i // 6, i % 6 + 1)
        return carry
    lax.fori_loop(0, 12, inside, 0)
    gram_y = multiply(halves, 1, 7)
    hand_on(2)
    arrive(straight_copies(2) + hand_waits(2))
    for s in range(2):
        for side, slab in sides_of_slab:
            take_rows(cell_v, s, side, slab, recv_rows[2][row_at[s][side]].astype(F32))
    for s in range(2):
        for y in (0, 7):
            halve(cell_v, halves, s, y)
    own_b = press(fold(gram_y + multiply(halves, 0, 1) + multiply(halves, 7, 8)))
    part_b[...] = own_b
    plane_copies_b = exchange(in_plane, part_b, plane_b, 2)
    start(plane_copies_b)
    own_b = collect(plane_copies_b, own_b, plane_b)
    mid_b[...] = own_b
    depth_copies_b = exchange(along_z, mid_b, depth_b, 3)
    start(depth_copies_b)

    def symmetric(total, count):
        turned = jnp.transpose(jnp.concatenate([total, jnp.zeros((96, 128), F32)], axis=0))
        return [
            jnp.where(lane32 < 32, 0.5 * (roll(total, -32 * m) + turned[32 * m:32 * m + 32]), 0.0) for m in range(count)
        ]

    row_id = lax.broadcasted_iota(jnp.int32, (64, 128), 0)

    def eliminate(system, first):
        for base in range(first, first + 32, 8):
            spreads = [jnp.broadcast_to(system[:, base + j:base + j + 1], (64, 128)) for j in range(8)]
            for j in range(8):
                k, column = base + j, spreads[j]
                scale = pl.reciprocal(column[k:k + 1, :])
                pivot = system[k:k + 1, :] * scale
                system = jnp.where(row_id == k, pivot, system - column * pivot)
                for m in range(j + 1, 8):
                    other = spreads[m][k:k + 1, :] * scale
                    spreads[m] = jnp.where(row_id == k, other, spreads[m] - column * other)
        return system

    own_a = collect(depth_copies_a, own_a, depth_a)
    s_mat, g_mat, h_mat = symmetric(sum(roll(spread(own_a[8 * m:8 * m + 8]), 32 * m) for m in range(3)), 3)
    system = jnp.concatenate([
        g_mat + roll(h_mat, 32) + roll(s_mat, 64),
        h_mat + roll(g_mat, 64),
    ], axis=0)
    system = eliminate(system, 0)
    own_b = collect(depth_copies_b, own_b, depth_b)
    (y_mat,) = symmetric(spread(own_b), 1)
    system = jnp.concatenate([system[0:32], system[32:64] + roll(y_mat, 32)], axis=0)
    system = eliminate(system, 32)
    mix = roll(jnp.where((lanes(64) >> 5) == 2, system, 0.0), 64)
    mix = mix + roll(mix, 32) + roll(mix, 64) + roll(mix, 96)
    pieces = [jnp.where((lane32 >> 5) == k, mix[32 * m:32 * m + 32], 0.0) for m in range(2) for k in range(4)]
    weights = jnp.concatenate([
        jnp.transpose(jnp.concatenate(pieces[0:4], axis=0)),
        jnp.transpose(jnp.concatenate(pieces[4:8], axis=0)),
    ], axis=1)
    weight_high, weight_low = split(weights)
    weight_both = jnp.concatenate([weight_high, weight_low], axis=0)
    across = (((1,), (1,)), ((), ()))

    def finish(s, y):
        row = pl.ds(pl.multiple_of(y * 128, 128), 128)
        high = jnp.concatenate([halves_b[s, row, 0:128], halves_q[s, row, 0:128]], axis=1)
        low = jnp.concatenate([halves_b[s, row, 128:256], halves_q[s, row, 128:256]], axis=1)
        first = lax.dot_general(weight_both, high, across, preferred_element_type=F32)
        second = lax.dot_general(weight_high, low, across, preferred_element_type=F32)
        value = first[0:128] + first[128:256] + second
        for k in range(4):
            result[pl.ds(s * 1024 + k * 8 + y, 32, stride=32), :] = value[32 * k:32 * k + 32]
    for pair in range(8):
        s, y = pair // 4, 2 * (pair % 4)
        row = slice(y * 128, y * 128 + 256)
        high = jnp.concatenate([halves_b[s, row, 0:128], halves_q[s, row, 0:128]], axis=1)
        low = jnp.concatenate([halves_b[s, row, 128:256], halves_q[s, row, 128:256]], axis=1)
        first = lax.dot_general(weight_both, high, across, preferred_element_type=F32)
        second = lax.dot_general(weight_high, low, across, preferred_element_type=F32)
        value = first[0:128] + first[128:256] + second
        for k in range(4):
            for t in range(2):
                result[pl.ds(s * 1024 + k * 8 + y + t, 32, stride=32), :] = value[32 * k:32 * k + 32, 128 * t:128 * t + 128]
    for kind in range(3):
        for copy in straight_copies(kind) + cross_copies(kind) + hand_copies(kind):
            copy.wait_send()
    for copy in col_copies(0) + relay_copies() + col_copies(1):
        copy.wait_send()
    for copy in plane_copies_a + depth_copies_a + plane_copies_b + depth_copies_b:
        copy.wait_send()


def on_device(click_field, roughness, slot_block, neighbours, density, class_kappa):
    hbm = pl.BlockSpec(memory_space=pltpu.HBM)
    vmem = pl.BlockSpec(memory_space=pltpu.VMEM)
    dma = pltpu.SemaphoreType.DMA
    answer = pl.pallas_call(
        kernel,
        out_shape=jax.ShapeDtypeStruct((2048, 128), F32),
        in_specs=[hbm] * 6,
        out_specs=vmem,
        scratch_shapes=[
            pltpu.SMEM((128,), jnp.int32),
            pltpu.SMEM((4, 64), jnp.int32),
            pltpu.SMEM((64,), jnp.int32),
            pltpu.SMEM((4,), F32),
            pltpu.VMEM((64, 128), F32),
            pltpu.VMEM((2048, 128), F32),
            pltpu.VMEM((2, 10, 144, 128), F32),
            pltpu.VMEM((2, 10, 144, 128), F32),
            pltpu.VMEM((2, 10, 144, 128), F32),
            pltpu.VMEM((2, 8, 128, 128), F32),
            pltpu.VMEM((2, 1024, 256), BF16),
            pltpu.VMEM((2, 1024, 256), BF16),
            pltpu.VMEM((2, 1024, 256), BF16),
            pltpu.VMEM((3, 2, 2, 32, 128), BF16),
            pltpu.VMEM((2, 32, 128), BF16),
            pltpu.VMEM((2, 16, 128), BF16),
            *[pltpu.VMEM((10, 32, 128), BF16) for _ in range(3)],
            pltpu.VMEM((8, 2, 32, 128), BF16),
            pltpu.VMEM((8, 2, 16, 128), BF16),
            pltpu.VMEM((2, 8, 128), F32),
            pltpu.VMEM((5, 8, 128), F32),
            pltpu.VMEM((24, 128), F32), pltpu.VMEM((8, 24, 128), F32),
            pltpu.VMEM((24, 128), F32), pltpu.VMEM((8, 24, 128), F32),
            pltpu.VMEM((8, 128), F32), pltpu.VMEM((8, 8, 128), F32),
            pltpu.VMEM((8, 128), F32), pltpu.VMEM((8, 8, 128), F32),
            dma((5,)), dma((2,)),
            dma((3, 5)), dma((3, 5)),
            dma((2, 8)), dma((2, 8)),
            dma((5,)), dma((5,)),
            dma((4, 8)), dma((4, 8)),
        ],
        compiler_params=pltpu.CompilerParams(
            collective_id=0, has_side_effects=True, vmem_limit_bytes=40 * 1024 * 1024),
        name="smooth",
    )(
        *[pltpu.with_memory_space_constraint(x, pltpu.HBM) for x in (
            slot_block, neighbours.T, density, class_kappa,
            click_field.reshape(2048, 128), roughness.reshape(64, 128))]
    )
    return answer.reshape(click_field.shape)


def solution(mesh):
    return jax.shard_map(
        on_device,
        mesh=mesh,
        in_specs=(
            P(("region", "blk"), None, None, None),
            P(("region", "blk"), None, None),
            P("region"),
            P("region", None),
            P("region"),
            P(),
        ),
        out_specs=P(("region", "blk"), None, None, None),
        check_vma=False,
    )
```

```python
import jax
import jax.numpy as jnp
from jax import lax
from jax.experimental import pallas as pl
from jax.experimental.pallas import tpu as pltpu
from jax.sharding import PartitionSpec as P

F32, BF16 = jnp.float32, jnp.bfloat16
MESH = pl.DeviceIdType.MESH


def lanes(rows):
    return lax.broadcasted_iota(jnp.int32, (rows, 128), 1)


def roll(value, shift):
    return value if shift % 128 == 0 else pltpu.roll(value, shift % 128, 1)


def split(value):
    high = value.astype(BF16)
    low = (value - high.astype(F32)).astype(BF16)
    return high, low


def kernel(
    slots_in, near_in, density_in, kappas_in, field, rough_in, result,
    slots, near, density, kappas, rough,
    staged, cell_b, cell_v, cell_q, diag, halves_b, halves_q, halves,
    send_rows, send_cols_0, send_cols_1, rows_b, rows_v, rows_q, cols_0, cols_1, send_relay, relays,
    part_a, plane_a, mid_a, depth_a, part_b, plane_b, mid_b, depth_b,
    table_sem, in_sem, row_send, row_recv, col_send, col_recv, relay_send, relay_recv, sum_send, sum_recv,
):
    send_cols, recv_cols = (send_cols_0, send_cols_1), (cols_0, cols_1)
    recv_rows = (rows_b, rows_v, rows_q)
    region, me = lax.axis_index("region"), lax.axis_index("blk")
    depth, spot = me // 8, me % 8
    half, inner = spot // 4, spot % 4
    low_half = depth < 4
    straight = lax.rem(me + 32, 64)
    crossing = jnp.where(depth == 0, 7, jnp.where(depth == 7, 0, jnp.where(low_half, depth + 3, depth - 3)))

    def device(number):
        return (region, number)

    def in_plane(step):
        return depth * 8 + lax.rem(spot + step, 8)

    def in_crossing(step):
        return crossing * 8 + half * 4 + lax.rem(inner + step, 4)

    def along_z(step):
        return lax.rem(depth + step, 8) * 8 + spot

    barrier = pltpu.get_barrier_semaphore()
    peers = [in_plane(k) for k in range(1, 8)] + [along_z(k) for k in range(1, 8)] + [in_crossing(k) for k in range(1, 4)]
    for peer in peers:
        pl.semaphore_signal(barrier, inc=1, device_id=device(peer), device_id_type=MESH)

    tables = [
        pltpu.make_async_copy(source, target, table_sem.at[i])
        for i, (source, target) in enumerate((
            (slots_in, slots), (near_in, near), (density_in, density), (kappas_in, kappas), (rough_in, rough)))
    ]
    for copy in tables:
        copy.start()
    load = [pltpu.make_async_copy(field.at[pl.ds(s * 1024, 1024)], staged.at[pl.ds(s * 1024, 1024)], in_sem.at[s]) for s in range(2)]
    for copy in load:
        copy.start()

    for copy in tables:
        copy.wait()
    blocks = [slots[me * 2 + s] for s in range(2)]
    filled = [b >= 0 for b in blocks]
    safe = [jnp.maximum(b, 0) for b in blocks]
    kappa = [kappas[density[b]] for b in safe]
    sides = [[jnp.where(filled[s], near[k, safe[s]], -1) for k in range(4)] for s in range(2)]
    plane_ids = [slots[depth * 16 + u] for u in range(16)]
    cross_ids = [slots[(crossing * 2 + half) * 8 + u] for u in range(8)]
    straight_ids = [slots[straight * 2 + u] for u in range(2)]

    def find(block, ids):
        place = jnp.int32(0)
        for u, candidate in enumerate(ids):
            place = jnp.where(candidate == block, u, place)
        return place

    def look(side, block):
        return jnp.where(block >= 0, near[side, jnp.maximum(block, 0)], -1)

    def first_of(*choices):
        answer = choices[-1]
        for choice in choices[-2::-1]:
            answer = jnp.where(choice >= 0, choice, answer)
        return answer

    def plane_place(block):
        u = find(block, plane_ids)
        return (spot - (u >> 1)) & 7, u & 1

    col_at, row_at, flank_at, relay_at, corner = [], [], [], [], []
    for s in range(2):
        here, north, south = blocks[s], sides[s][2], sides[s][3]
        col_at.append([plane_place(sides[s][k]) for k in range(2)])
        flank_at.append([
            plane_place(first_of(sides[s][k], look(3, look(k, north)), look(2, look(k, south)))) for k in range(2)
        ])
        far = jnp.where(low_half, north, south)
        close = jnp.where(low_half, south, north)
        u, v = find(far, cross_ids), find(close, straight_ids)
        far_step, far_slot = (inner - (u >> 1)) & 3, u & 1
        spots = (u, 8 + v)
        places = ((far_step, far_slot), (jnp.int32(4), v))
        row_at.append((jnp.where(low_half, spots[0], spots[1]), jnp.where(low_half, spots[1], spots[0])))
        relay_at.append([
            tuple(jnp.where(low_half, places[side][i], places[1 - side][i]) for i in range(2)) for side in range(2)
        ])
        corner.append([[
            jnp.where(beyond >= 0, jnp.where(look(k, beyond) >= 0, 1.0, 0.0) + jnp.where(sides[s][k] >= 0, 1.0, 0.0), 0.0)
            for k in range(2)] for beyond in (north, south)])

    crossing_side = jnp.where(low_half, 0, 1)

    core, chip = inner % 2, inner // 2
    sibling = in_plane(1 - 2 * core + 8)

    def remote(source, target, send, recv, number):
        return pltpu.make_async_remote_copy(source, target, send, recv, device_id=device(number), device_id_type=MESH)

    def cross_copies(kind):
        source = send_rows.at[kind, crossing_side]
        target = recv_rows[kind].at[pl.ds(2 * inner, 2)]
        return [
            remote(source, target, row_send.at[kind, k], row_recv.at[kind, chip],
                   crossing * 8 + half * 4 + 2 * k + core)
            for k in range(2)
        ]

    def cross_waits(kind):
        return [
            remote(send_rows.at[kind, crossing_side], recv_rows[kind].at[pl.ds(2 * (2 * k + core), 2)],
                   row_send.at[kind, k], row_recv.at[kind, k], sibling)
            for k in range(2)
        ]

    def straight_copies(kind):
        return [remote(send_rows.at[kind, 1 - crossing_side], recv_rows[kind].at[pl.ds(8, 2)],
                       row_send.at[kind, 2], row_recv.at[kind, 2], straight)]

    def hand_copies(kind):
        return [
            remote(recv_rows[kind].at[pl.ds(2 * (2 * k + core), 2)], recv_rows[kind].at[pl.ds(2 * (2 * k + core), 2)],
                   row_send.at[kind, 3 + k], row_recv.at[kind, 3 + k], sibling)
            for k in range(2)
        ]

    def hand_waits(kind):
        return [
            remote(recv_rows[kind].at[pl.ds(2 * (2 * k + core), 2)], recv_rows[kind].at[pl.ds(2 * (2 * k + 1 - core), 2)],
                   row_send.at[kind, 3 + k], row_recv.at[kind, 3 + k], sibling)
            for k in range(2)
        ]

    def send_row_strips(kind):
        start(cross_copies(kind) + straight_copies(kind))

    def hand_on(kind):
        arrive(cross_waits(kind))
        start(hand_copies(kind))

    def relay_copies():
        return [
            remote(send_relay.at[crossing_side], relays.at[k], relay_send.at[k], relay_recv.at[k], in_crossing(k))
            for k in range(4)
        ] + [remote(send_relay.at[1 - crossing_side], relays.at[4], relay_send.at[4], relay_recv.at[4], straight)]

    def col_copies(level):
        return [
            pltpu.make_async_remote_copy(
                send_cols[level], recv_cols[level].at[k],
                col_send.at[level, k], col_recv.at[level, k],
                device_id=device(in_plane(k)), device_id_type=MESH)
            for k in range(1, 8)
        ]

    lane32, lane128 = lanes(32), lanes(128)

    sides_of_slab = ((0, 1), (1, 8))

    def packed(cells, s, side, slab):
        answer = jnp.zeros((32, 128), F32)
        for k in range(4):
            piece = roll(cells[s, slab, 8 + 32 * k:40 + 32 * k, :], 32 * k - 96 * side)
            answer = jnp.where((lane32 >> 5) == k, piece, answer)
        return answer.astype(BF16)

    def columns(cells, s):
        return [cells[s, 1 + y, row:row + 1, :] for row in (8, 135) for y in range(8)]

    def send_columns(level, s, rows):
        strip = jnp.concatenate(rows, axis=0).astype(BF16)
        send_cols[level][s] = strip
        recv_cols[level][0, s] = strip

    def start(copies):
        for copy in copies:
            copy.start()

    def arrive(copies):
        for copy in copies:
            copy.wait_recv()

    def linked(s, k):
        return sides[s][k] >= 0

    def column_of(level, s, k, first):
        step, slot = col_at[s][k]
        strip = recv_cols[level][step, slot].astype(F32)
        return strip[first + 8:first + 16] if k == 0 else strip[first:first + 8]

    def take_columns(cells, s, k, strip):
        row = (8, 135)[k]
        strip = jnp.where(linked(s, k), strip, 0.0)
        for y in range(8):
            cells[s, 1 + y, row:row + 1, :] = cells[s, 1 + y, row:row + 1, :] - strip[y:y + 1]

    def take_rows(cells, s, side, slab, strip, back=None):
        touching = (lane32 >> 5) == 3 * side
        for k in range(4):
            rows = slice(8 + 32 * k, 40 + 32 * k)
            piece = roll(strip, 96 * side - 32 * k)
            if back is not None:
                piece = piece - back[s, slab, rows, :]
            piece = jnp.where(touching, jnp.where(linked(s, 2 + side), piece, 0.0), 0.0)
            cells[s, slab, rows, :] = cells[s, slab, rows, :] - piece

    def send_relays():
        top = lax.broadcasted_iota(jnp.int32, (8, 128), 0)
        lane8 = lanes(8)
        found = []
        for s in range(2):
            (west_step, west_slot), (east_step, east_slot) = flank_at[s]
            found.append((
                recv_cols[0][west_step, west_slot].astype(F32)[8:16],
                recv_cols[0][east_step, east_slot].astype(F32)[0:8],
            ))
        for side in range(2):
            lines = []
            for west, east in found:
                row = slice(7 * side, 7 * side + 1)
                line = jnp.where(lanes(1) < 32, roll(west[row], 32 * side), roll(east[row], 32 + 32 * side))
                lines.append(jnp.broadcast_to(line, (8, 128)))
            value = jnp.where(top == 0, lines[0], lines[1])
            send_relay[side] = jnp.where(lane8 < 64, value, 0.0)
        start(relay_copies())

    def take_corners(cells):
        for s in range(2):
            for side, slab in sides_of_slab:
                index, slot = relay_at[s][side]
                tile = relays[index]
                line = jnp.where(slot == 0, tile[0:1], tile[1:2])
                for k, row in ((0, 8), (1, 135)):
                    factor = corner[s][side][k]
                    value = jnp.where(factor > 0.0, roll(line, 96 * side - 32 * k) * factor, 0.0)
                    value = jnp.where((lanes(1) >> 5) == 3 * side, value, 0.0)
                    cells[s, slab, row:row + 1, :] = cells[s, slab, row:row + 1, :] + value

    def wrap(cells):
        for s in range(2):
            cells[s, 0, 8:136, :] = jnp.where(lane128 < 32, 0.0, roll(cells[s, 8, 8:136, :], 32))
            cells[s, 9, 8:136, :] = jnp.where(lane128 >= 96, 0.0, roll(cells[s, 1, 8:136, :], 96))

    def each_slab(body, unroll=8):
        def step(i, carry):
            body(i >> 3, i & 7)
            return carry
        lax.fori_loop(0, 16, step, 0, unroll=unroll)

    def operate(source, target):
        def body(s, y):
            centre = source[s, y + 1, 8:136, :]
            beside = source[s, y + 1, 7:135, :] + source[s, y + 1, 9:137, :]
            along = source[s, y, 8:136, :] + source[s, y + 2, 8:136, :]
            target[s, y + 1, 8:136, :] = diag[s, y] * centre - (beside + along)
        each_slab(body)

    def multiply(parts, first, last):
        total = jnp.zeros((128, 256), F32)
        for s in range(2):
            rows = slice(first * 128, last * 128)
            total = total + lax.dot_general(
                parts[s, rows, 0:128], parts[s, rows, :], (((0,), (0,)), ((), ())), preferred_element_type=F32)
        return total

    def halve(cells, parts, s, y):
        high, low = split(cells[s, y + 1, 8:136, :])
        row = pl.ds(pl.multiple_of(y * 128, 128), 128)
        parts[s, row, 0:128] = high
        parts[s, row, 128:256] = low

    def fold(total):
        total = total[:, 0:128] + 2.0 * total[:, 128:256]
        answer = total[0:32]
        for k in range(1, 4):
            answer = answer + roll(total[32 * k:32 * k + 32], -32 * k)
        return jnp.where(lane32 < 32, answer, 0.0)

    def gram(cells, parts):
        each_slab(lambda s, y: halve(cells, parts, s, y))
        return fold(multiply(parts, 0, 8))

    def press(value):
        answer = value[0:8]
        for k in range(1, 4):
            answer = answer + roll(value[8 * k:8 * k + 8], 32 * k)
        return answer

    def spread(value):
        return jnp.concatenate([jnp.where(lanes(8) < 32, roll(value, -32 * k), 0.0) for k in range(4)], axis=0)

    def exchange(peer, source, target, index):
        return [
            pltpu.make_async_remote_copy(
                source, target.at[k], sum_send.at[index, k], sum_recv.at[index, k],
                device_id=device(peer(k)), device_id_type=MESH)
            for k in range(1, 8)
        ]

    def collect(copies, own, target):
        for k, copy in enumerate(copies):
            copy.wait_recv()
            own = own + target[k + 1]
        return own

    blank = jnp.zeros((8, 128), F32)
    for cells in (cell_b, cell_v, cell_q):
        for s in range(2):
            for y in range(10):
                cells[s, y, 0:8, :] = blank
                cells[s, y, 136:144, :] = blank

    def fill_diag(s, y):
        value = jnp.where(s == 0, kappa[0], kappa[1])
        rows = [jnp.broadcast_to(rough[pl.ds(s * 32 + k * 8 + y, 1), :], (32, 128)) for k in range(4)]
        diag[s, y] = jnp.transpose(jnp.concatenate(rows, axis=0)) * value + 4.0
    each_slab(fill_diag)

    for copy in load:
        copy.wait()

    def turn(s, y):
        keep = jnp.where(s == 0, blocks[0], blocks[1]) >= 0
        rows = [staged[pl.ds(s * 1024 + k * 8 + y, 32, stride=32), :] for k in range(4)]
        cell_b[s, y + 1, 8:136, :] = jnp.where(keep, jnp.transpose(jnp.concatenate(rows, axis=0)), 0.0)
    each_slab(turn)

    wrap(cell_b)
    operate(cell_b, cell_v)
    for s in range(2):
        for side, slab in sides_of_slab:
            send_rows[0, side, s] = packed(cell_b, s, side, slab)
            send_rows[1, side, s] = packed(cell_v, s, side, slab)
        send_columns(0, s, columns(cell_b, s) + columns(cell_v, s))
    pl.semaphore_wait(barrier, len(peers))
    start(cross_copies(0) + straight_copies(0) + col_copies(0) + cross_copies(1) + straight_copies(1))
    gram_s = gram(cell_b, halves_b)
    arrive(col_copies(0))
    send_relays()
    for s in range(2):
        for k in range(2):
            take_columns(cell_v, s, k, column_of(0, s, k, 0))
    hand_on(0)
    arrive(straight_copies(0) + hand_waits(0))
    for s in range(2):
        for side, slab in sides_of_slab:
            take_rows(cell_v, s, side, slab, recv_rows[0][row_at[s][side]].astype(F32))
    hand_on(1)
    wrap(cell_v)
    operate(cell_v, cell_q)
    for s in range(2):
        for k in range(2):
            back = jnp.concatenate(columns(cell_b, s)[8 * k:8 * k + 8], axis=0)
            take_columns(cell_q, s, k, column_of(0, s, k, 16) - back)
    arrive(relay_copies())
    take_corners(cell_q)
    arrive(straight_copies(1) + hand_waits(1))
    for s in range(2):
        for side, slab in sides_of_slab:
            take_rows(cell_q, s, side, slab, recv_rows[1][row_at[s][side]].astype(F32), cell_b)
    for s in range(2):
        for side, slab in sides_of_slab:
            send_rows[2, side, s] = packed(cell_q, s, side, slab)
    send_row_strips(2)
    for s in range(2):
        send_columns(1, s, columns(cell_q, s))
    start(col_copies(1))
    gram_g = gram(cell_v, halves)

    gram_h = gram(cell_q, halves_q)
    own_a = jnp.concatenate([press(gram_s), press(gram_g), press(gram_h)], axis=0)
    part_a[...] = own_a
    plane_copies_a = exchange(in_plane, part_a, plane_a, 0)
    start(plane_copies_a)
    wrap(cell_q)
    operate(cell_q, cell_v)
    arrive(col_copies(1))
    for s in range(2):
        for k in range(2):
            take_columns(cell_v, s, k, column_of(1, s, k, 0))

    def inside(i, carry):
        halve(cell_v, halves, i // 6, i % 6 + 1)
        return carry
    lax.fori_loop(0, 12, inside, 0)
    gram_y = multiply(halves, 1, 7)
    own_a = collect(plane_copies_a, own_a, plane_a)
    mid_a[...] = own_a
    depth_copies_a = exchange(along_z, mid_a, depth_a, 1)
    start(depth_copies_a)
    hand_on(2)
    arrive(straight_copies(2) + hand_waits(2))
    for s in range(2):
        for side, slab in sides_of_slab:
            take_rows(cell_v, s, side, slab, recv_rows[2][row_at[s][side]].astype(F32))
    for s in range(2):
        for y in (0, 7):
            halve(cell_v, halves, s, y)
    own_b = press(fold(gram_y + multiply(halves, 0, 1) + multiply(halves, 7, 8)))
    part_b[...] = own_b
    plane_copies_b = exchange(in_plane, part_b, plane_b, 2)
    start(plane_copies_b)
    own_b = collect(plane_copies_b, own_b, plane_b)
    mid_b[...] = own_b
    depth_copies_b = exchange(along_z, mid_b, depth_b, 3)
    start(depth_copies_b)

    def symmetric(total, count):
        turned = jnp.transpose(jnp.concatenate([total, jnp.zeros((96, 128), F32)], axis=0))
        return [
            jnp.where(lane32 < 32, 0.5 * (roll(total, -32 * m) + turned[32 * m:32 * m + 32]), 0.0) for m in range(count)
        ]

    row_id = lax.broadcasted_iota(jnp.int32, (64, 128), 0)

    def eliminate(system, first):
        for base in range(first, first + 32, 8):
            spreads = [jnp.broadcast_to(system[:, base + j:base + j + 1], (64, 128)) for j in range(8)]
            for j in range(8):
                k, column = base + j, spreads[j]
                scale = pl.reciprocal(column[k:k + 1, :])
                pivot = system[k:k + 1, :] * scale
                system = jnp.where(row_id == k, pivot, system - column * pivot)
                for m in range(j + 1, 8):
                    other = spreads[m][k:k + 1, :] * scale
                    spreads[m] = jnp.where(row_id == k, other, spreads[m] - column * other)
        return system

    own_a = collect(depth_copies_a, own_a, depth_a)
    s_mat, g_mat, h_mat = symmetric(sum(roll(spread(own_a[8 * m:8 * m + 8]), 32 * m) for m in range(3)), 3)
    system = jnp.concatenate([
        g_mat + roll(h_mat, 32) + roll(s_mat, 64),
        h_mat + roll(g_mat, 64),
    ], axis=0)
    system = eliminate(system, 0)
    own_b = collect(depth_copies_b, own_b, depth_b)
    (y_mat,) = symmetric(spread(own_b), 1)
    system = jnp.concatenate([system[0:32], system[32:64] + roll(y_mat, 32)], axis=0)
    system = eliminate(system, 32)
    mix = roll(jnp.where((lanes(64) >> 5) == 2, system, 0.0), 64)
    mix = mix + roll(mix, 32) + roll(mix, 64) + roll(mix, 96)
    pieces = [jnp.where((lane32 >> 5) == k, mix[32 * m:32 * m + 32], 0.0) for m in range(2) for k in range(4)]
    weights = jnp.concatenate([
        jnp.transpose(jnp.concatenate(pieces[0:4], axis=0)),
        jnp.transpose(jnp.concatenate(pieces[4:8], axis=0)),
    ], axis=1)
    weight_high, weight_low = split(weights)
    weight_both = jnp.concatenate([weight_high, weight_low], axis=0)
    across = (((1,), (1,)), ((), ()))

    def finish(s, y):
        row = pl.ds(pl.multiple_of(y * 128, 128), 128)
        high = jnp.concatenate([halves_b[s, row, 0:128], halves_q[s, row, 0:128]], axis=1)
        low = jnp.concatenate([halves_b[s, row, 128:256], halves_q[s, row, 128:256]], axis=1)
        first = lax.dot_general(weight_both, high, across, preferred_element_type=F32)
        second = lax.dot_general(weight_high, low, across, preferred_element_type=F32)
        value = first[0:128] + first[128:256] + second
        for k in range(4):
            result[pl.ds(s * 1024 + k * 8 + y, 32, stride=32), :] = value[32 * k:32 * k + 32]
    for pair in range(8):
        s, y = pair // 4, 2 * (pair % 4)
        row = slice(y * 128, y * 128 + 256)
        high = jnp.concatenate([halves_b[s, row, 0:128], halves_q[s, row, 0:128]], axis=1)
        low = jnp.concatenate([halves_b[s, row, 128:256], halves_q[s, row, 128:256]], axis=1)
        first = lax.dot_general(weight_both, high, across, preferred_element_type=F32)
        second = lax.dot_general(weight_high, low, across, preferred_element_type=F32)
        value = first[0:128] + first[128:256] + second
        for k in range(4):
            for t in range(2):
                result[pl.ds(s * 1024 + k * 8 + y + t, 32, stride=32), :] = value[32 * k:32 * k + 32, 128 * t:128 * t + 128]
    for kind in range(3):
        for copy in straight_copies(kind) + cross_copies(kind) + hand_copies(kind):
            copy.wait_send()
    for copy in col_copies(0) + relay_copies() + col_copies(1):
        copy.wait_send()
    for copy in plane_copies_a + depth_copies_a + plane_copies_b + depth_copies_b:
        copy.wait_send()


def on_device(click_field, roughness, slot_block, neighbours, density, class_kappa):
    hbm = pl.BlockSpec(memory_space=pltpu.HBM)
    vmem = pl.BlockSpec(memory_space=pltpu.VMEM)
    dma = pltpu.SemaphoreType.DMA
    answer = pl.pallas_call(
        kernel,
        out_shape=jax.ShapeDtypeStruct((2048, 128), F32),
        in_specs=[hbm] * 6,
        out_specs=vmem,
        scratch_shapes=[
            pltpu.SMEM((128,), jnp.int32),
            pltpu.SMEM((4, 64), jnp.int32),
            pltpu.SMEM((64,), jnp.int32),
            pltpu.SMEM((4,), F32),
            pltpu.VMEM((64, 128), F32),
            pltpu.VMEM((2048, 128), F32),
            pltpu.VMEM((2, 10, 144, 128), F32),
            pltpu.VMEM((2, 10, 144, 128), F32),
            pltpu.VMEM((2, 10, 144, 128), F32),
            pltpu.VMEM((2, 8, 128, 128), F32),
            pltpu.VMEM((2, 1024, 256), BF16),
            pltpu.VMEM((2, 1024, 256), BF16),
            pltpu.VMEM((2, 1024, 256), BF16),
            pltpu.VMEM((3, 2, 2, 32, 128), BF16),
            pltpu.VMEM((2, 32, 128), BF16),
            pltpu.VMEM((2, 16, 128), BF16),
            *[pltpu.VMEM((10, 32, 128), BF16) for _ in range(3)],
            pltpu.VMEM((8, 2, 32, 128), BF16),
            pltpu.VMEM((8, 2, 16, 128), BF16),
            pltpu.VMEM((2, 8, 128), F32),
            pltpu.VMEM((5, 8, 128), F32),
            pltpu.VMEM((24, 128), F32), pltpu.VMEM((8, 24, 128), F32),
            pltpu.VMEM((24, 128), F32), pltpu.VMEM((8, 24, 128), F32),
            pltpu.VMEM((8, 128), F32), pltpu.VMEM((8, 8, 128), F32),
            pltpu.VMEM((8, 128), F32), pltpu.VMEM((8, 8, 128), F32),
            dma((5,)), dma((2,)),
            dma((3, 5)), dma((3, 5)),
            dma((2, 8)), dma((2, 8)),
            dma((5,)), dma((5,)),
            dma((4, 8)), dma((4, 8)),
        ],
        compiler_params=pltpu.CompilerParams(
            collective_id=0, has_side_effects=True, vmem_limit_bytes=40 * 1024 * 1024),
        name="smooth",
    )(
        *[pltpu.with_memory_space_constraint(x, pltpu.HBM) for x in (
            slot_block, neighbours.T, density, class_kappa,
            click_field.reshape(2048, 128), roughness.reshape(64, 128))]
    )
    return answer.reshape(click_field.shape)


def solution(mesh):
    return jax.shard_map(
        on_device,
        mesh=mesh,
        in_specs=(
            P(("region", "blk"), None, None, None),
            P(("region", "blk"), None, None),
            P("region"),
            P("region", None),
            P("region"),
            P(),
        ),
        out_specs=P(("region", "blk"), None, None, None),
        check_vma=False,
    )
```
